512 devices in a mesh: dp: 16 (over y_lo, x, core), expert: 4 (over y_hi), tensor: 8 (over z).
Axes of the slice: x: 4, y: 8 (y_hi: 4, y_lo: 2; y = y_hi * 2 + y_lo), z: 8, core: 2. Of those that a mesh axis runs over, the one named last changes fastest.
Arguments:
- tokens: bfloat16 [1792, 4096], P(('dp', 'expert'), 'tensor'), may hold values from -6 to 6
- route_ids: int32 [1792, 2], P(('dp', 'expert')), may hold values from 0 to 3, all different within a row; in each aligned block of 28 rows (0 to 27, 28 to 55, ...) at most 17 rows name the same one
- route_gates: float32 [1792, 2], P(('dp', 'expert')), may hold values from 0.2 to 1
- d_out: bfloat16 [1792, 4096], P(('dp', 'expert'), 'tensor'), may hold values from -6 to 6
- gate_saved: bfloat16 [4, 4096, 8192], P(None, 'tensor', ('dp', 'expert')), may hold values from -0.09375 to 0.09375
- up_saved: bfloat16 [4, 4096, 8192], P(None, 'tensor', ('dp', 'expert')), may hold values from -0.09375 to 0.09375
- down_saved: bfloat16 [4, 4096, 8192], P(None, 'tensor', ('dp', 'expert')), may hold values from -0.0625 to 0.0625
Outputs:
- out: bfloat16 [1792, 4096], P(('dp', 'expert'), 'tensor')
- d_tokens: bfloat16 [1792, 4096], P(('dp', 'expert'), 'tensor')
- grad_gate: bfloat16 [4, 4096, 8192], P('expert', 'tensor', 'dp')
- grad_up: bfloat16 [4, 4096, 8192], P('expert', 'tensor', 'dp')
- grad_down: bfloat16 [4, 4096, 8192], P('expert', 'tensor', 'dp')
The draws below stay inside these ranges and needn't reach their ends.
Inputs may be any that keep to these rules, and one draw needn't show every extreme that they name: `route_ids`: each token names two different experts. Among the 28 tokens of one aligned block of the token dimension no expert is named more than 17 times, and in some block one expert is named exactly 17 times.
All inputs are finite; a program needn't handle non-finite values.
Results may differ from the reference program's by a relative error of at most 0.028.
Values may be sent and summed in bfloat16 or wider, within the bound.
No kernel may reach another device: no remote copies, remote signals or barrier semaphores. Data moves between devices by JAX's collectives and lax.ppermute only.
A program may use at most 64 MiB of HBM per device.

```python
import math
import jax
import jax.numpy as jnp
import numpy as np
from jax import lax

D = 4096
FF = 8192
TOK_DEV = 28
EXPERTS = 4
CAP = 17
TOKENS = 1792
ROWS = 1088
N_DP = 16
N_EXPERT = 4
N_TENSOR = 8


def block_levels(key, dims, shards, low, high):
    loudness = 1.0
    for position, blocks in shards:
        draws = jax.random.uniform(jax.random.fold_in(jax.random.fold_in(key, 6), position), (blocks,), jnp.float32, low / len(shards), high / len(shards))
        loudness = loudness * jnp.repeat(jnp.exp(draws), dims[position] // blocks).reshape((-1,) + (1,) * (len(dims) - 1 - position))
    return loudness


def routed_block(stream_key, own, number, rows, count, top, reach, lean):
    sequence = jax.random.permutation(stream_key, count)
    heavy_load, common = load_shares(count, rows * top, reach, lean, True), load_shares(count, rows * top, reach, lean, False)
    places = jnp.arange(count)

    def named(sizes, rotation):
        used = int((sizes > 0).sum())
        fixed = max(1, used // 4)
        moved = fixed + (places - fixed + rotation * (used - fixed)) % max(1, count - fixed)
        return jnp.zeros((count,), jnp.int32).at[sequence[jnp.where(places < fixed, places, moved)]].set(jnp.asarray(sizes, jnp.int32))

    sizes = jnp.where(number % 4 == 0, named(heavy_load, number // 4), named(common, number - number // 4 - 1))
    mixed = jax.random.permutation(jax.random.fold_in(own, 3), count)
    giver, sink = mixed[0:count // 2 * 2:2], mixed[1:count // 2 * 2:2]
    margin = jnp.minimum(sizes[giver] - 1, reach - sizes[sink]) // 2
    margin = jnp.where((giver == sequence[0]) | (sink == sequence[0]) | (sizes[sink] == 0), 0, jnp.maximum(margin, 0))
    moved = jax.random.randint(jax.random.fold_in(own, 4), (count // 2,), 0, 1 << 20) % (margin + 1)
    sizes = sizes.at[giver].add(-moved).at[sink].add(moved)
    labels = jnp.searchsorted(jnp.cumsum(sizes), jnp.arange(rows * top), side="right").astype(jnp.int32)
    grid = labels.reshape(top, rows).T
    grid = grid[jax.random.permutation(jax.random.fold_in(own, 1), rows)]
    rotation = jax.random.randint(jax.random.fold_in(own, 2), (rows, 1), 0, top)
    return jnp.take_along_axis(grid, (jnp.arange(top)[None, :] + rotation) % top, axis=1)


def load_shares(number_of, total, reach, skew, full):
    loads = [(1 << 20) // math.isqrt(standing ** skew) + 1 for standing in range(1, number_of + 1)]
    largest = reach if full else min(reach, max(-(-total // number_of), total * loads[0] // sum(loads)))
    least = 1 if total - largest >= number_of - 1 else 0
    given, rest = [largest] + [least] * (number_of - 1), total - largest - least * (number_of - 1)
    while rest > 0:
        candidates = [i for i in range(1, number_of) if given[i] < largest] or [i for i in range(1, number_of) if given[i] < reach]
        whole, left = sum([loads[i] for i in candidates]), rest
        for i in candidates:
            more = min(reach - given[i], max(1, left * loads[i] // whole), rest)
            given[i] = given[i] + more
            rest = rest - more
    return np.array(given)


def centred(own_key, shape, scale, reach, pieces=(), kind=jnp.bfloat16):
    array = jax.random.normal(own_key, shape, jnp.float32) * scale
    if len(pieces) > 0:
        array = block_levels(own_key, shape, pieces, -0.22, 0.18) * array
    return jnp.clip(array, min=-reach, max=reach).astype(kind)


def setup_inputs(seed: int = 0) -> dict:
    keys = jax.random.split(jax.random.key(seed), 8)
    tokens = centred(keys[0], (TOKENS, D), 1.0, 6.0, ((0, 64), (1, 8)))
    route_ids_keys = jax.random.split(jax.random.fold_in(keys[1], 1), TOKENS // TOK_DEV)
    route_ids_turns = jax.random.permutation(jax.random.fold_in(keys[1], 3), TOKENS // TOK_DEV)
    route_ids = jax.vmap(lambda own, number: routed_block(jax.random.fold_in(keys[1], 2), own, number, TOK_DEV, N_EXPERT, 2, CAP, 2))(route_ids_keys, route_ids_turns).reshape((TOKENS, 2))
    route_gates = jnp.clip(0.2 + 0.8 * jax.random.uniform(keys[2], (TOKENS, 2), jnp.float32) ** block_levels(keys[2], (TOKENS, 2), ((0, 64),), -0.2, 0.2), 0.2, 1.0)
    d_out = centred(keys[3], (TOKENS, D), 1.0, 6.0, ((0, 64), (1, 8)))
    gate_saved = centred(keys[4], (EXPERTS, D, FF), D ** -0.5, 0.09375, ((1, 8), (2, 64)))
    up_saved = centred(keys[5], (EXPERTS, D, FF), D ** -0.5, 0.09375, ((1, 8), (2, 64)))
    down_saved = centred(keys[6], (EXPERTS, D, FF), FF ** -0.5, 0.0625, ((1, 8), (2, 64)))
    return dict(tokens=tokens, route_ids=route_ids, route_gates=route_gates, d_out=d_out, gate_saved=gate_saved, up_saved=up_saved, down_saved=down_saved)


def swiglu_pair(gate_sum, up_sum, back_sum):
    sigmoid_gate = jax.nn.sigmoid(gate_sum)
    silu_gate = gate_sum * sigmoid_gate
    hidden = (silu_gate * up_sum).astype(jnp.bfloat16)
    d_up = (back_sum * silu_gate).astype(jnp.bfloat16)
    d_gate = (back_sum * up_sum * sigmoid_gate * (1.0 + gate_sum * (1.0 - sigmoid_gate))).astype(jnp.bfloat16)
    return hidden, d_gate, d_up


def block_sum(rows_in, weight):
    width_part = D // N_TENSOR
    running = jnp.zeros((rows_in.shape[0], weight.shape[1]), jnp.float32)
    for block_index in range(N_TENSOR):
        lower = block_index * width_part
        upper = lower + width_part
        partial_product = jnp.dot(rows_in[:, lower:upper], weight[lower:upper], preferred_element_type=jnp.float32)
        rounded = lax.optimization_barrier(partial_product.astype(jnp.bfloat16))
        running = running + rounded.astype(jnp.float32)
    return running


def contract_rows(left_side, right_side):
    return lax.dot_general(left_side, right_side, (((0,), (0,)), ((), ())), preferred_element_type=jnp.float32)


def contract_last(left_side, right_side):
    return lax.dot_general(left_side, right_side, (((1,), (1,)), ((), ())), preferred_element_type=jnp.float32)


def hidden_block_sum(pairs):
    hidden_part = FF // N_DP
    running = jnp.zeros((pairs[0][0].shape[0], pairs[0][1].shape[0]), jnp.float32)
    for block_index in range(N_DP):
        lower = block_index * hidden_part
        upper = lower + hidden_part
        partial_product = jnp.zeros_like(running)
        for left_side, right_side in pairs:
            partial_product = partial_product + contract_last(left_side[:, lower:upper], right_side[:, lower:upper])
        rounded = lax.optimization_barrier(partial_product.astype(jnp.bfloat16))
        running = running + rounded.astype(jnp.float32)
    return running


def expert_pass(operands):
    rows_x, rows_dy, w_gate, w_up, w_down = operands
    gate_sum = block_sum(rows_x, w_gate)
    up_sum = block_sum(rows_x, w_up)
    back_sum = block_sum(rows_dy, w_down)
    hidden, d_gate, d_up = swiglu_pair(gate_sum, up_sum, back_sum)
    expert_out = hidden_block_sum(((hidden, w_down),)).astype(jnp.bfloat16)
    expert_dx = hidden_block_sum(((d_gate, w_gate), (d_up, w_up))).astype(jnp.bfloat16)
    grad_gate = contract_rows(rows_x, d_gate).astype(jnp.bfloat16)
    grad_up = contract_rows(rows_x, d_up).astype(jnp.bfloat16)
    grad_down = contract_rows(rows_dy, hidden).astype(jnp.bfloat16)
    return expert_out, expert_dx, grad_gate, grad_up, grad_down


def reference(tokens, route_ids, route_gates, d_out, gate_saved, up_saved, down_saved):
    blocks = TOKENS // TOK_DEV
    block_ids = route_ids.reshape(blocks, TOK_DEV, 2)
    onehot = (block_ids[..., None] == jnp.arange(EXPERTS, dtype=jnp.int32)).astype(jnp.int32)
    flat_hits = onehot.reshape(blocks, TOK_DEV * 2, EXPERTS)
    before = (jnp.cumsum(flat_hits, axis=1) - flat_hits).astype(jnp.int32)
    slot_index = jnp.sum(before * flat_hits, axis=2).astype(jnp.int32).reshape(blocks, TOK_DEV, 2)
    row_index = (jnp.arange(blocks, dtype=jnp.int32)[:, None, None] * CAP + slot_index).astype(jnp.int32)
    token_blocks = tokens.reshape(blocks, TOK_DEV, 1, D)
    token_copies = jnp.broadcast_to(token_blocks, (blocks, TOK_DEV, 2, D))
    gates = route_gates.reshape(blocks, TOK_DEV, 2, 1)
    gated_dy = (gates * d_out.reshape(blocks, TOK_DEV, 1, D).astype(jnp.float32)).astype(jnp.bfloat16)
    rows_x = jnp.zeros((EXPERTS, ROWS, D), jnp.bfloat16).at[block_ids, row_index].set(token_copies)
    rows_dy = jnp.zeros((EXPERTS, ROWS, D), jnp.bfloat16).at[block_ids, row_index].set(gated_dy)
    expert_out, expert_dx, grad_gate, grad_up, grad_down = lax.map(
        expert_pass, (rows_x, rows_dy, gate_saved, up_saved, down_saved))
    picked_out = expert_out[block_ids, row_index].astype(jnp.float32)
    picked_dx = expert_dx[block_ids, row_index].astype(jnp.float32)
    out = jnp.sum(gates * picked_out, axis=2).reshape(TOKENS, D).astype(jnp.bfloat16)
    d_tokens = jnp.sum(picked_dx, axis=2).reshape(TOKENS, D).astype(jnp.bfloat16)
    return out, d_tokens, grad_gate, grad_up, grad_down
```

```python
import functools

import jax
import jax.numpy as jnp
from jax import lax
from jax.experimental import pallas as pl
from jax.experimental.pallas import tpu as pltpu
from jax.sharding import Mesh, PartitionSpec as P


CHIPS = ("ylo", "x")
BF16 = jnp.bfloat16
F32 = jnp.float32


def place_of(ids_row, expert, slots):
    tokens = ids_row.shape[1]
    hits = jnp.sum((ids_row == expert).astype(F32), axis=0, keepdims=True)
    earlier = (
        lax.broadcasted_iota(jnp.int32, (tokens, tokens), 0)
        < lax.broadcasted_iota(jnp.int32, (tokens, tokens), 1)
    ).astype(F32)
    before = jnp.dot(
        jnp.broadcast_to(hits, (8, tokens)), earlier, preferred_element_type=F32
    )[:1].astype(jnp.int32)
    slot = lax.broadcasted_iota(jnp.int32, (slots, tokens), 0)
    return jnp.where((slot == before) & (hits > 0.5), 1.0, 0.0).astype(F32)


def send_kernel(ids_ref, gates_ref, tok_ref, dout_ref, out_ref):
    experts, slots = out_ref.shape[0] // 2, out_ref.shape[1]
    ids, gates = ids_ref[...], gates_ref[...]
    for e in range(experts):
        place = place_of(ids, e, slots)
        gate_row = jnp.sum(jnp.where(ids == e, gates, 0.0), axis=0, keepdims=True)
        gate_slot = jnp.sum(place * gate_row, axis=1, keepdims=True)
        pick = place.astype(BF16)
        out_ref[e] = jnp.dot(pick, tok_ref[...], preferred_element_type=F32).astype(BF16)
        grads = jnp.dot(pick, dout_ref[...], preferred_element_type=F32)
        out_ref[experts + e] = (gate_slot * grads).astype(BF16)


def finish_kernel(ids_ref, gates_ref, back_ref, out_ref, dtok_ref):
    experts, slots = back_ref.shape[0] // 2, back_ref.shape[1]
    ids, gates = ids_ref[...], gates_ref[...]
    tokens = ids.shape[1]
    eye = lax.broadcasted_iota(jnp.int32, (tokens, tokens), 0) == lax.broadcasted_iota(
        jnp.int32, (tokens, tokens), 1
    )
    out = jnp.zeros(out_ref.shape, F32)
    dtok = jnp.zeros(dtok_ref.shape, F32)
    for e in range(experts):
        pick = place_of(ids, e, slots).astype(BF16)
        gate_row = jnp.sum(jnp.where(ids == e, gates, 0.0), axis=0, keepdims=True)
        gate_col = jnp.sum(jnp.where(eye, gate_row, 0.0), axis=1, keepdims=True)
        spread = functools.partial(
            lax.dot_general,
            pick,
            dimension_numbers=(((0,), (0,)), ((), ())),
            preferred_element_type=F32,
        )
        out += gate_col * spread(back_ref[e])
        dtok += spread(back_ref[experts + e])
    out_ref[...] = out.astype(BF16)
    dtok_ref[...] = dtok.astype(BF16)


def pack_kernel(expert_ref, *refs):
    saved, outs = refs[:3], refs[3:]
    width = saved[0].shape[2]
    for r, out in enumerate(outs):

        @pl.when(pl.program_id(0) == r)
        def _():
            for a in range(3):
                out[:, a * width : (a + 1) * width] = saved[a][0]


def pack(expert, saved):
    n, depth, width = saved[0].shape
    return pl.pallas_call(
        pack_kernel,
        grid_spec=pltpu.PrefetchScalarGridSpec(
            num_scalar_prefetch=1,
            grid=(n,),
            in_specs=[pl.BlockSpec((1, depth, width), lambda i, e: ((e[0] + i) & (n - 1), 0, 0))] * 3,
            out_specs=[pl.BlockSpec((depth, 3 * width), lambda i, e: (0, 0))] * n,
        ),
        out_shape=[jax.ShapeDtypeStruct((depth, 3 * width), BF16)] * n,
        cost_estimate=pl.CostEstimate(
            flops=0, bytes_accessed=12 * n * depth * width, transcendentals=0
        ),
    )(expert.astype(jnp.int32).reshape(1), *saved)


def place_kernel(expert_ref, *refs):
    pieces, out = refs[:-1], refs[-1]
    width = out.shape[2]
    for r, piece in enumerate(pieces):

        @pl.when(pl.program_id(0) == r)
        def _():
            for a in range(3):
                out[a] = piece[:, a * width : (a + 1) * width]


def place(expert, pieces):
    n, (depth, width3) = len(pieces), pieces[0].shape
    width = width3 // 3
    return pl.pallas_call(
        place_kernel,
        grid_spec=pltpu.PrefetchScalarGridSpec(
            num_scalar_prefetch=1,
            grid=(n,),
            in_specs=[pl.BlockSpec((depth, width3), lambda i, e: (0, 0))] * n,
            out_specs=pl.BlockSpec((3, depth, width), lambda i, e: (0, 0, (e[0] - i) & (n - 1))),
        ),
        out_shape=jax.ShapeDtypeStruct((3, depth, n * width), BF16),
        cost_estimate=pl.CostEstimate(
            flops=0, bytes_accessed=12 * n * depth * width, transcendentals=0
        ),
    )(expert.astype(jnp.int32).reshape(1), *pieces)


def part_kernel(n, order_ref, mine_x_ref, other_x_ref, w_ref, *out_refs):
    width = w_ref.shape[2]
    first = order_ref[1] == 0
    mine, other = mine_x_ref[0], other_x_ref[0]
    x, dy = jnp.where(first, mine, other), jnp.where(first, other, mine)

    def fill(outs):
        for a, rows in enumerate((x, x, dy)):
            s = slice(a * width, (a + 1) * width)
            product = jnp.dot(rows, w_ref[a], preferred_element_type=F32).astype(BF16)
            lower = 0
            for out in outs:
                out[:, s] = product[lower : lower + out.shape[0]]
                lower += out.shape[0]

    if n == 1:
        fill(out_refs)
        return
    for i, out in enumerate(out_refs):
        pl.when(pl.program_id(0) == i)(functools.partial(fill, (out,)))


def stepper(steps, ring):
    first, jump = steps[0], steps[-1] - steps[0]
    return lambda i, o: (o[0] + first + jump * i) & (ring - 1)


def parts(where, steps, mine, other, w, heights=None):
    ring, height, depth = mine.shape
    width = w.shape[2]
    n = len(steps)
    chunk = stepper(steps, ring)
    heights = heights or (height,) * n
    return pl.pallas_call(
        functools.partial(part_kernel, n),
        grid_spec=pltpu.PrefetchScalarGridSpec(
            num_scalar_prefetch=1,
            grid=(n,),
            in_specs=[
                pl.BlockSpec((1, height, depth), lambda i, o: (chunk(i, o), 0, 0)),
                pl.BlockSpec((1, height, depth), lambda i, o: (chunk(i, o), 0, 0)),
                pl.BlockSpec(w.shape, lambda i, o: (0, 0, 0)),
            ],
            out_specs=[pl.BlockSpec((h, 3 * width), lambda i, o: (0, 0)) for h in heights],
        ),
        out_shape=[jax.ShapeDtypeStruct((h, 3 * width), BF16) for h in heights],
        cost_estimate=pl.CostEstimate(
            flops=n * height * depth * width * 6,
            bytes_accessed=2 * (n * height * (2 * depth + 3 * width) + 3 * depth * width),
            transcendentals=0,
        ),
    )(where, mine, other, w)


def act_kernel(a_ref, b_ref, c_ref, out_ref):
    width = a_ref.shape[1] // 3

    def total(k):
        s = slice(k * width, (k + 1) * width)
        return a_ref[:, s].astype(F32) + b_ref[:, s].astype(F32) + c_ref[:, s].astype(F32)

    gate, up, back = total(0), total(1), total(2)
    sig = jax.nn.sigmoid(gate)
    silu = gate * sig
    out_ref[:, :width] = (back * up * sig * (1.0 + gate * (1.0 - sig))).astype(BF16)
    out_ref[:, width : 2 * width] = (back * silu).astype(BF16)
    out_ref[:, 2 * width :] = (silu * up).astype(BF16)


def contract_last(left, right):
    return lax.dot_general(
        left, right, (((1,), (1,)), ((), ())), preferred_element_type=F32
    )


def back_rows(acts, first, w_ref, keep_ref, send_ref, all_ref, lower, upper):
    width = w_ref.shape[2]
    d_gate, d_up, hidden = (acts[:, k * width : (k + 1) * width] for k in range(3))
    out = contract_last(hidden, w_ref[2])
    d_x = contract_last(d_gate, w_ref[0]) + contract_last(d_up, w_ref[1])
    keep_ref[0, lower:upper] = jnp.where(first, out, d_x).astype(BF16)
    send_ref[0, lower:upper] = jnp.where(first, d_x, out).astype(BF16)
    all_ref[0, lower:upper] = acts


def back_kernel(n, halves, order_ref, *refs):
    chunks, w_ref = refs[:n], refs[n]
    outs = refs[-3:]
    first = order_ref[1] == 0
    if halves:
        lower = 0
        for c in chunks:
            back_rows(c[...], first, w_ref, *outs, lower, lower + c.shape[0])
            lower += c.shape[0]
        return
    for i, c in enumerate(chunks):

        @pl.when(pl.program_id(0) == i)
        def _():
            back_rows(c[...], first, w_ref, *outs, 0, c.shape[0])


def back(where, steps, chunks, w, held, n_chunks, halves=False):
    n = len(chunks)
    chunk = stepper(steps, n_chunks)
    height = sum(c.shape[0] for c in chunks) if halves else chunks[0].shape[0]
    width3 = chunks[0].shape[1]
    depth = w.shape[1]
    grid = len(steps)
    in_specs = [pl.BlockSpec(c.shape, lambda i, o: (0, 0)) for c in chunks]
    in_specs.append(pl.BlockSpec(w.shape, lambda i, o: (0, 0, 0)))
    aliases = {}
    extra = ()
    if held is not None:
        in_specs += [pl.BlockSpec(memory_space=pl.ANY)] * 3
        aliases = {n + 2: 0, n + 3: 1, n + 4: 2}
        extra = held
    return pl.pallas_call(
        functools.partial(back_kernel, n, halves),
        grid_spec=pltpu.PrefetchScalarGridSpec(
            num_scalar_prefetch=1,
            grid=(grid,),
            in_specs=in_specs,
            out_specs=[
                pl.BlockSpec((1, height, depth), lambda i, o: (chunk(i, o), 0, 0)),
                pl.BlockSpec((1, height, depth), lambda i, o: (chunk(i, o), 0, 0)),
                pl.BlockSpec((1, height, width3), lambda i, o: (chunk(i, o), 0, 0)),
            ],
        ),
        out_shape=[
            jax.ShapeDtypeStruct((n_chunks, height, depth), BF16),
            jax.ShapeDtypeStruct((n_chunks, height, depth), BF16),
            jax.ShapeDtypeStruct((n_chunks, height, width3), BF16),
        ],
        input_output_aliases=aliases,
        cost_estimate=pl.CostEstimate(
            flops=grid * height * depth * width3 * 2,
            bytes_accessed=2 * (grid * height * (2 * width3 + 2 * depth) + depth * width3),
            transcendentals=0,
        ),
    )(where, *chunks, w, *extra)


def contract_rows(left, right):
    return lax.dot_general(
        left, right, (((0,), (0,)), ((), ())), preferred_element_type=F32
    )


def step(tokens, route_ids, route_gates, d_out, gate_saved, up_saved, down_saved):
    experts = lax.axis_size("expert")
    ring = lax.axis_size("tensor")
    n_chips = lax.axis_size("ylo") * lax.axis_size("x")
    tok_count, depth = tokens.shape
    slots = 5 * tok_count // 8
    part = gate_saved.shape[2]
    width = experts * part
    core = lax.axis_index("core")

    ids_row, gates_row = route_ids.T, route_gates.T
    sent = pl.pallas_call(
        send_kernel,
        out_shape=jax.ShapeDtypeStruct((2 * experts, slots, depth), BF16),
    )(ids_row, gates_row, tokens, d_out)
    own = lax.all_to_all(sent, ("core", "expert"), 0, 0, tiled=True)
    height = 2 * experts * slots
    own = own.reshape(height, depth)
    expert = lax.axis_index("expert")
    pieces = pack(expert, (gate_saved, up_saved, down_saved))
    pieces = [pieces[0]] + [
        lax.ppermute(pieces[r], "expert", [(i, (i + r) % experts) for i in range(experts)])
        for r in range(1, experts)
    ]
    w = place(expert, pieces)
    mine = lax.all_to_all(
        jnp.broadcast_to(own[None], (n_chips, height, depth)), CHIPS, 0, 0, tiled=True
    )
    swap = [(0, 1), (1, 0)]
    other = lax.ppermute(mine, "core", swap)

    right = [(i, (i + 1) % ring) for i in range(ring)]
    left = [(i, (i - 1) % ring) for i in range(ring)]
    here = lax.axis_index("tensor")

    def both(to_right, to_left):
        return (lax.ppermute(to_right, "tensor", right), lax.ppermute(to_left, "tensor", left))

    where = jnp.stack([here, core]).astype(jnp.int32)

    half = height // 16 * 8
    got = both(*parts(where, (4,), mine, other, w, (half, height - half)))
    own_r, own_l = parts(where, (3, -3,), mine, other, w)
    to_right = jnp.concatenate((own_r[:half] + got[0], own_r[half:]), axis=0)
    to_left = jnp.concatenate((own_l[:half], own_l[half:] + got[1]), axis=0)
    for k in (2, 1):
        got = both(to_right, to_left)
        own_r, own_l = parts(where, (k, -k,), mine, other, w)
        to_right, to_left = got[0] + own_r, got[1] + own_l
    got = both(to_right, to_left)
    (own_0,) = parts(where, (0,), mine, other, w)
    acts = pl.pallas_call(
        act_kernel, out_shape=jax.ShapeDtypeStruct((height, 3 * width), BF16)
    )(own_0, *got)

    got = both(acts, acts)
    held = back(where, (0,), (acts,), w, None, ring)
    for k in (1, 2, 3):
        now = got
        if k < 3:
            got = both(*now)
        else:
            got = both(now[0][:half], now[1][half:])
        held = back(where, (-k, k,), now, w, held, ring)
    keep, send, acts = back(where, (4,), got, w, held, ring, halves=True)

    got = lax.ppermute(send, "core", swap)
    sums = (keep.astype(F32) + got.astype(F32)).astype(BF16)
    sums = lax.all_to_all(sums, CHIPS, 0, 0, tiled=True)
    own = jnp.sum(sums.astype(F32), axis=0).astype(BF16)
    own = own.reshape(2 * experts, slots, depth)
    returned = lax.all_to_all(own, ("core", "expert"), 0, 0, tiled=True)
    out, d_tokens = pl.pallas_call(
        finish_kernel,
        out_shape=[jax.ShapeDtypeStruct(tokens.shape, BF16)] * 2,
    )(ids_row, gates_row, returned)

    acts = acts.reshape(ring * height, 3 * width)
    x = jnp.where(core == 0, mine, other).reshape(n_chips * height, depth)
    dy = jnp.where(core == 0, other, mine).reshape(n_chips * height, depth)
    grads = [
        contract_rows(x if a < 2 else dy, acts[:, a * width : (a + 1) * width]).astype(BF16)[None]
        for a in range(3)
    ]
    return (out, d_tokens, *grads)


def solution(mesh):
    fine = Mesh(
        mesh.devices.reshape(2, 4, 2, 4, 8), ("ylo", "x", "core", "expert", "tensor")
    )
    dp = ("ylo", "x", "core")
    tok = P((*dp, "expert"), "tensor")
    route = P((*dp, "expert"), None)
    saved = P(None, "tensor", (*dp, "expert"))
    grad = P("expert", "tensor", dp)
    return jax.shard_map(
        step,
        mesh=fine,
        in_specs=(tok, route, route, tok, saved, saved, saved),
        out_specs=(tok, tok, grad, grad, grad),
        check_vma=False,
    )
```

```python
import functools

import jax
import jax.numpy as jnp
from jax import lax
from jax.experimental import pallas as pl
from jax.experimental.pallas import tpu as pltpu
from jax.sharding import Mesh, PartitionSpec as P


NEAR = ("ylo", "core", "expert")
BF16 = jnp.bfloat16
F32 = jnp.float32
call = functools.partial(
    pl.pallas_call, compiler_params=pltpu.CompilerParams(vmem_limit_bytes=14 << 20)
)


def place_of(ids_row, expert, slots):
    tokens = ids_row.shape[1]
    hits = jnp.sum((ids_row == expert).astype(F32), axis=0, keepdims=True)
    earlier = (
        lax.broadcasted_iota(jnp.int32, (tokens, tokens), 0)
        < lax.broadcasted_iota(jnp.int32, (tokens, tokens), 1)
    ).astype(F32)
    before = jnp.dot(
        jnp.broadcast_to(hits, (8, tokens)), earlier, preferred_element_type=F32
    )[:1].astype(jnp.int32)
    slot = lax.broadcasted_iota(jnp.int32, (slots, tokens), 0)
    return jnp.where((slot == before) & (hits > 0.5), 1.0, 0.0).astype(F32)


def send_kernel(ids_ref, gates_ref, tok_ref, dout_ref, out_ref):
    copies, both, slots, _ = out_ref.shape
    experts = both // 2
    ids, gates = ids_ref[...], gates_ref[...]
    for e in range(experts):
        place = place_of(ids, e, slots)
        gate_row = jnp.sum(jnp.where(ids == e, gates, 0.0), axis=0, keepdims=True)
        gate_slot = jnp.sum(place * gate_row, axis=1, keepdims=True)
        pick = place.astype(BF16)
        rows = jnp.dot(pick, tok_ref[...], preferred_element_type=F32).astype(BF16)
        grads = jnp.dot(pick, dout_ref[...], preferred_element_type=F32)
        grads = (gate_slot * grads).astype(BF16)
        for c in range(copies):
            out_ref[c, e] = rows
            out_ref[c, experts + e] = grads


def finish_kernel(ids_ref, gates_ref, back_ref, out_ref, dtok_ref):
    copies, both, slots, _ = back_ref.shape
    experts = both // 2
    ids, gates = ids_ref[...], gates_ref[...]
    tokens = ids.shape[1]

    def returned(k):
        return sum(back_ref[c, k].astype(F32) for c in range(copies)).astype(BF16)

    eye = lax.broadcasted_iota(jnp.int32, (tokens, tokens), 0) == lax.broadcasted_iota(
        jnp.int32, (tokens, tokens), 1
    )
    out = jnp.zeros(out_ref.shape, F32)
    dtok = jnp.zeros(dtok_ref.shape, F32)
    for e in range(experts):
        pick = place_of(ids, e, slots).astype(BF16)
        gate_row = jnp.sum(jnp.where(ids == e, gates, 0.0), axis=0, keepdims=True)
        gate_col = jnp.sum(jnp.where(eye, gate_row, 0.0), axis=1, keepdims=True)
        spread = functools.partial(
            lax.dot_general,
            pick,
            dimension_numbers=(((0,), (0,)), ((), ())),
            preferred_element_type=F32,
        )
        out += gate_col * spread(returned(e))
        dtok += spread(returned(experts + e))
    out_ref[...] = out.astype(BF16)
    dtok_ref[...] = dtok.astype(BF16)


def pack_kernel(expert_ref, *refs):
    saved, outs = refs[:3], refs[3:]
    width = saved[0].shape[2]
    for r, out in enumerate(outs):

        @pl.when(pl.program_id(0) == r)
        def _():
            for a in range(3):
                out[:, a * width : (a + 1) * width] = saved[a][0]


def pack(expert, saved):
    n, depth, width = saved[0].shape
    return call(
        pack_kernel,
        grid_spec=pltpu.PrefetchScalarGridSpec(
            num_scalar_prefetch=1,
            grid=(n,),
            in_specs=[pl.BlockSpec((1, depth, width), lambda i, e: ((e[0] + i) & (n - 1), 0, 0))] * 3,
            out_specs=[pl.BlockSpec((depth, 3 * width), lambda i, e: (0, 0))] * n,
        ),
        out_shape=[jax.ShapeDtypeStruct((depth, 3 * width), BF16)] * n,
        cost_estimate=pl.CostEstimate(
            flops=0, bytes_accessed=12 * n * depth * width, transcendentals=0
        ),
    )(expert.astype(jnp.int32).reshape(1), *saved)


def place_kernel(expert_ref, *refs):
    pieces, out = refs[:-1], refs[-1]
    width = out.shape[2]
    for r, piece in enumerate(pieces):

        @pl.when(pl.program_id(0) == r)
        def _():
            for a in range(3):
                out[a] = piece[:, a * width : (a + 1) * width]


def place(expert, pieces):
    n, (depth, width3) = len(pieces), pieces[0].shape
    width = width3 // 3
    return call(
        place_kernel,
        grid_spec=pltpu.PrefetchScalarGridSpec(
            num_scalar_prefetch=1,
            grid=(n,),
            in_specs=[pl.BlockSpec((depth, width3), lambda i, e: (0, 0))] * n,
            out_specs=pl.BlockSpec((3, depth, width), lambda i, e: (0, 0, (e[0] - i) & (n - 1))),
        ),
        out_shape=jax.ShapeDtypeStruct((3, depth, n * width), BF16),
        cost_estimate=pl.CostEstimate(
            flops=0, bytes_accessed=12 * n * depth * width, transcendentals=0
        ),
    )(expert.astype(jnp.int32).reshape(1), *pieces)


def part_kernel(n, order_ref, mine_x_ref, other_x_ref, w_ref, *out_refs):
    width = w_ref.shape[2]
    first = order_ref[1] == 0
    mine, other = mine_x_ref[0], other_x_ref[0]
    x, dy = jnp.where(first, mine, other), jnp.where(first, other, mine)

    def fill(outs):
        for a, rows in enumerate((x, x, dy)):
            s = slice(a * width, (a + 1) * width)
            product = jnp.dot(rows, w_ref[a], preferred_element_type=F32).astype(BF16)
            lower = 0
            for out in outs:
                out[:, s] = product[lower : lower + out.shape[0]]
                lower += out.shape[0]

    if n == 1:
        fill(out_refs)
        return
    for i, out in enumerate(out_refs):
        pl.when(pl.program_id(0) == i)(functools.partial(fill, (out,)))


def stepper(steps, ring):
    if len(steps) > 2:
        return lambda i, o: (o[0] + (steps[0] - (i >> 1)) * (1 - 2 * (i & 1))) & (ring - 1)
    first, jump = steps[0], steps[-1] - steps[0]
    return lambda i, o: (o[0] + first + jump * i) & (ring - 1)


def parts(where, steps, mine, other, w, heights=None):
    ring, height, depth = mine.shape
    width = w.shape[2]
    n = len(steps)
    chunk = stepper(steps, ring)
    heights = heights or (height,) * n
    return call(
        functools.partial(part_kernel, n),
        grid_spec=pltpu.PrefetchScalarGridSpec(
            num_scalar_prefetch=1,
            grid=(n,),
            in_specs=[
                pl.BlockSpec((1, height, depth), lambda i, o: (chunk(i, o), 0, 0)),
                pl.BlockSpec((1, height, depth), lambda i, o: (chunk(i, o), 0, 0)),
                pl.BlockSpec(w.shape, lambda i, o: (0, 0, 0)),
            ],
            out_specs=[pl.BlockSpec((h, 3 * width), lambda i, o: (0, 0)) for h in heights],
        ),
        out_shape=[jax.ShapeDtypeStruct((h, 3 * width), BF16) for h in heights],
        cost_estimate=pl.CostEstimate(
            flops=n * height * depth * width * 6,
            bytes_accessed=2 * (n * height * (2 * depth + 3 * width) + 3 * depth * width),
            transcendentals=0,
        ),
    )(where, mine, other, w)


def merge_kernel(lower, own_ref, got_ref, out_ref):
    upper = lower + got_ref.shape[0]
    if lower:
        out_ref[:lower] = own_ref[:lower]
    if upper < out_ref.shape[0]:
        out_ref[upper:] = own_ref[upper:]
    out_ref[lower:upper] = own_ref[lower:upper] + got_ref[...]


def merge(own, got, lower):
    return call(
        functools.partial(merge_kernel, lower),
        out_shape=jax.ShapeDtypeStruct(own.shape, BF16),
        cost_estimate=pl.CostEstimate(
            flops=own.size, bytes_accessed=6 * own.size, transcendentals=0
        ),
    )(own, got)


def act_kernel(a_ref, b_ref, c_ref, out_ref):
    width = a_ref.shape[1] // 3

    def total(k):
        s = slice(k * width, (k + 1) * width)
        return a_ref[:, s].astype(F32) + b_ref[:, s].astype(F32) + c_ref[:, s].astype(F32)

    gate, up, back = total(0), total(1), total(2)
    sig = jax.nn.sigmoid(gate)
    silu = gate * sig
    out_ref[:, :width] = (back * up * sig * (1.0 + gate * (1.0 - sig))).astype(BF16)
    out_ref[:, width : 2 * width] = (back * silu).astype(BF16)
    out_ref[:, 2 * width :] = (silu * up).astype(BF16)


def contract_last(left, right):
    return lax.dot_general(
        left, right, (((1,), (1,)), ((), ())), preferred_element_type=F32
    )


def back_rows(acts, first, w_ref, keep_ref, send_ref, all_ref, lower, upper):
    width = w_ref.shape[2]
    d_gate, d_up, hidden = (acts[:, k * width : (k + 1) * width] for k in range(3))
    out = contract_last(hidden, w_ref[2])
    d_x = contract_last(d_gate, w_ref[0]) + contract_last(d_up, w_ref[1])
    keep_ref[0, lower:upper] = jnp.where(first, out, d_x).astype(BF16)
    send_ref[0, lower:upper] = jnp.where(first, d_x, out).astype(BF16)
    all_ref[0, lower:upper] = acts


def back_kernel(n, halves, order_ref, *refs):
    chunks, w_ref = refs[:n], refs[n]
    outs = refs[-3:]
    first = order_ref[1] == 0
    if halves:
        lower = 0
        for c in chunks:
            back_rows(c[...], first, w_ref, *outs, lower, lower + c.shape[0])
            lower += c.shape[0]
        return
    for i, c in enumerate(chunks):

        @pl.when(pl.program_id(0) == i)
        def _():
            back_rows(c[...], first, w_ref, *outs, 0, c.shape[0])


def back(where, steps, chunks, w, held, n_chunks, halves=False):
    n = len(chunks)
    chunk = stepper(steps, n_chunks)
    height = sum(c.shape[0] for c in chunks) if halves else chunks[0].shape[0]
    width3 = chunks[0].shape[1]
    depth = w.shape[1]
    grid = len(steps)
    in_specs = [pl.BlockSpec(c.shape, lambda i, o: (0, 0)) for c in chunks]
    in_specs.append(pl.BlockSpec(w.shape, lambda i, o: (0, 0, 0)))
    aliases = {}
    extra = ()
    if held is not None:
        in_specs += [pl.BlockSpec(memory_space=pl.ANY)] * 3
        aliases = {n + 2: 0, n + 3: 1, n + 4: 2}
        extra = held
    return call(
        functools.partial(back_kernel, n, halves),
        grid_spec=pltpu.PrefetchScalarGridSpec(
            num_scalar_prefetch=1,
            grid=(grid,),
            in_specs=in_specs,
            out_specs=[
                pl.BlockSpec((1, height, depth), lambda i, o: (chunk(i, o), 0, 0)),
                pl.BlockSpec((1, height, depth), lambda i, o: (chunk(i, o), 0, 0)),
                pl.BlockSpec((1, height, width3), lambda i, o: (chunk(i, o), 0, 0)),
            ],
        ),
        out_shape=[
            jax.ShapeDtypeStruct((n_chunks, height, depth), BF16),
            jax.ShapeDtypeStruct((n_chunks, height, depth), BF16),
            jax.ShapeDtypeStruct((n_chunks, height, width3), BF16),
        ],
        input_output_aliases=aliases,
        cost_estimate=pl.CostEstimate(
            flops=grid * height * depth * width3 * 2,
            bytes_accessed=2 * (grid * height * (2 * width3 + 2 * depth) + depth * width3),
            transcendentals=0,
        ),
    )(where, *chunks, w, *extra)


def split_kernel(sums_ref, out_ref):
    slots = out_ref.shape[1]
    total = sum(sums_ref[k].astype(F32) for k in range(sums_ref.shape[0])).astype(BF16)
    for k in range(out_ref.shape[0]):
        out_ref[k] = total[k * slots : (k + 1) * slots]


def contract_rows(left, right):
    return lax.dot_general(
        left, right, (((0,), (0,)), ((), ())), preferred_element_type=F32
    )


def step(tokens, route_ids, route_gates, d_out, gate_saved, up_saved, down_saved):
    experts = lax.axis_size("expert")
    ring = lax.axis_size("tensor")
    n_chips = lax.axis_size("ylo") * lax.axis_size("x")
    tok_count, depth = tokens.shape
    slots = 5 * tok_count // 8
    part = gate_saved.shape[2]
    width = experts * part
    core = lax.axis_index("core")

    ids_row, gates_row = route_ids.T, route_gates.T
    lows = lax.axis_size("ylo")
    sent = pl.pallas_call(
        send_kernel,
        out_shape=jax.ShapeDtypeStruct((lows, 2 * experts, slots, depth), BF16),
    )(ids_row, gates_row, tokens, d_out)
    height = 2 * experts * slots
    own = lax.all_to_all(
        sent.reshape(lows * 2 * experts, slots, depth), NEAR, 0, 0, tiled=True
    ).reshape(lows * height, depth)
    expert = lax.axis_index("expert")
    pieces = pack(expert, (gate_saved, up_saved, down_saved))
    pieces = [pieces[0]] + [
        lax.ppermute(pieces[r], "expert", [(i, (i + r) % experts) for i in range(experts)])
        for r in range(1, experts)
    ]
    w = place(expert, pieces)
    mine = lax.all_to_all(
        jnp.broadcast_to(own[None], (n_chips // lows, lows * height, depth)), "x", 0, 0, tiled=True
    ).reshape(n_chips, height, depth)
    swap = [(0, 1), (1, 0)]
    other = lax.ppermute(mine, "core", swap)

    right = [(i, (i + 1) % ring) for i in range(ring)]
    left = [(i, (i - 1) % ring) for i in range(ring)]
    here = lax.axis_index("tensor")

    def both(to_right, to_left):
        return (lax.ppermute(to_right, "tensor", right), lax.ppermute(to_left, "tensor", left))

    where = jnp.stack([here, core]).astype(jnp.int32)

    half = height // 16 * 8
    far = parts(where, (4,), mine, other, w, (half, height - half))
    got = both(*far)
    near = parts(where, (3, -3), mine, other, w)
    to_right = merge(near[0], got[0], 0)
    to_left = merge(near[1], got[1], half)
    got = both(to_right, to_left)
    near = parts(where, (2, -2, 1, -1, 0), mine, other, w)
    got = both(got[0] + near[0], got[1] + near[1])
    got = both(got[0] + near[2], got[1] + near[3])
    acts = call(
        act_kernel, out_shape=jax.ShapeDtypeStruct((height, 3 * width), BF16)
    )(near[4], *got)

    got = both(acts, acts)
    held = back(where, (0,), (acts,), w, None, ring)
    for k in (1, 2, 3):
        now = got
        if k < 3:
            got = both(*now)
        else:
            got = both(now[0][:half], now[1][half:])
        held = back(where, (-k, k,), now, w, held, ring)
    keep, send, acts = back(where, (4,), got, w, held, ring, halves=True)

    got = lax.ppermute(send, "core", swap)
    sums = (keep.astype(F32) + got.astype(F32)).astype(BF16)
    sums = sums.reshape(n_chips // lows, lows * height, depth)
    sums = lax.all_to_all(sums, "x", 0, 0, tiled=True)
    own = call(
        split_kernel,
        out_shape=jax.ShapeDtypeStruct((lows * 2 * experts, slots, depth), BF16),
    )(sums)
    returned = lax.all_to_all(own, NEAR, 0, 0, tiled=True)
    returned = returned.reshape(lows, 2 * experts, slots, depth)
    out, d_tokens = call(
        finish_kernel,
        out_shape=[jax.ShapeDtypeStruct(tokens.shape, BF16)] * 2,
    )(ids_row, gates_row, returned)

    acts = acts.reshape(ring * height, 3 * width)
    x = jnp.where(core == 0, mine, other).reshape(n_chips * height, depth)
    dy = jnp.where(core == 0, other, mine).reshape(n_chips * height, depth)
    grads = [
        contract_rows(x if a < 2 else dy, acts[:, a * width : (a + 1) * width]).astype(BF16)[None]
        for a in range(3)
    ]
    return (out, d_tokens, *grads)


def solution(mesh):
    fine = Mesh(
        mesh.devices.reshape(2, 4, 2, 4, 8), ("ylo", "x", "core", "expert", "tensor")
    )
    dp = ("ylo", "x", "core")
    tok = P((*dp, "expert"), "tensor")
    route = P((*dp, "expert"), None)
    saved = P(None, "tensor", (*dp, "expert"))
    grad = P("expert", "tensor", dp)
    return jax.shard_map(
        step,
        mesh=fine,
        in_specs=(tok, route, route, tok, saved, saved, saved),
        out_specs=(tok, tok, grad, grad, grad),
        check_vma=False,
    )
```

```python
import functools

import jax
import jax.numpy as jnp
from jax import lax
from jax.experimental import pallas as pl
from jax.experimental.pallas import tpu as pltpu
from jax.sharding import Mesh, PartitionSpec as P


NEAR = ("ylo", "core", "expert")
BF16 = jnp.bfloat16
F32 = jnp.float32
call = functools.partial(
    pl.pallas_call, compiler_params=pltpu.CompilerParams(vmem_limit_bytes=14 << 20)
)


def place_of(ids_row, expert, slots):
    tokens = ids_row.shape[1]
    hits = jnp.sum((ids_row == expert).astype(F32), axis=0, keepdims=True)
    earlier = (
        lax.broadcasted_iota(jnp.int32, (tokens, tokens), 0)
        < lax.broadcasted_iota(jnp.int32, (tokens, tokens), 1)
    ).astype(F32)
    before = jnp.dot(
        jnp.broadcast_to(hits, (8, tokens)), earlier, preferred_element_type=F32
    )[:1].astype(jnp.int32)
    slot = lax.broadcasted_iota(jnp.int32, (slots, tokens), 0)
    return jnp.where((slot == before) & (hits > 0.5), 1.0, 0.0).astype(F32)


def send_kernel(ids_ref, gates_ref, tok_ref, dout_ref, out_ref):
    copies, both, slots, _ = out_ref.shape
    experts = both // 2
    ids, gates = ids_ref[...], gates_ref[...]
    for e in range(experts):
        place = place_of(ids, e, slots)
        gate_row = jnp.sum(jnp.where(ids == e, gates, 0.0), axis=0, keepdims=True)
        gate_slot = jnp.sum(place * gate_row, axis=1, keepdims=True)
        pick = place.astype(BF16)
        rows = jnp.dot(pick, tok_ref[...], preferred_element_type=F32).astype(BF16)
        grads = jnp.dot(pick, dout_ref[...], preferred_element_type=F32)
        grads = (gate_slot * grads).astype(BF16)
        for c in range(copies):
            out_ref[c, e] = rows
            out_ref[c, experts + e] = grads


def finish_kernel(ids_ref, gates_ref, back_ref, out_ref, dtok_ref):
    experts, slots = back_ref.shape[0] // 2, back_ref.shape[1]
    ids, gates = ids_ref[...], gates_ref[...]
    tokens = ids.shape[1]
    eye = lax.broadcasted_iota(jnp.int32, (tokens, tokens), 0) == lax.broadcasted_iota(
        jnp.int32, (tokens, tokens), 1
    )
    out = jnp.zeros(out_ref.shape, F32)
    dtok = jnp.zeros(dtok_ref.shape, F32)
    for e in range(experts):
        pick = place_of(ids, e, slots).astype(BF16)
        gate_row = jnp.sum(jnp.where(ids == e, gates, 0.0), axis=0, keepdims=True)
        gate_col = jnp.sum(jnp.where(eye, gate_row, 0.0), axis=1, keepdims=True)
        spread = functools.partial(
            lax.dot_general,
            pick,
            dimension_numbers=(((0,), (0,)), ((), ())),
            preferred_element_type=F32,
        )
        out += gate_col * spread(back_ref[e])
        dtok += spread(back_ref[experts + e])
    out_ref[...] = out.astype(BF16)
    dtok_ref[...] = dtok.astype(BF16)


def pack_kernel(expert_ref, *refs):
    saved, outs = refs[:3], refs[3:]
    width = saved[0].shape[2]
    for r, out in enumerate(outs):

        @pl.when(pl.program_id(0) == r)
        def _():
            for a in range(3):
                out[:, a * width : (a + 1) * width] = saved[a][0]


def pack(expert, saved):
    n, depth, width = saved[0].shape
    return call(
        pack_kernel,
        grid_spec=pltpu.PrefetchScalarGridSpec(
            num_scalar_prefetch=1,
            grid=(n,),
            in_specs=[pl.BlockSpec((1, depth, width), lambda i, e: ((e[0] + i) & (n - 1), 0, 0))] * 3,
            out_specs=[pl.BlockSpec((depth, 3 * width), lambda i, e: (0, 0))] * n,
        ),
        out_shape=[jax.ShapeDtypeStruct((depth, 3 * width), BF16)] * n,
        cost_estimate=pl.CostEstimate(
            flops=0, bytes_accessed=12 * n * depth * width, transcendentals=0
        ),
    )(expert.astype(jnp.int32).reshape(1), *saved)


def place_kernel(expert_ref, *refs):
    pieces, out = refs[:-1], refs[-1]
    width = out.shape[2]
    for r, piece in enumerate(pieces):

        @pl.when(pl.program_id(0) == r)
        def _():
            for a in range(3):
                out[a] = piece[:, a * width : (a + 1) * width]


def place(expert, pieces):
    n, (depth, width3) = len(pieces), pieces[0].shape
    width = width3 // 3
    return call(
        place_kernel,
        grid_spec=pltpu.PrefetchScalarGridSpec(
            num_scalar_prefetch=1,
            grid=(n,),
            in_specs=[pl.BlockSpec((depth, width3), lambda i, e: (0, 0))] * n,
            out_specs=pl.BlockSpec((3, depth, width), lambda i, e: (0, 0, (e[0] - i) & (n - 1))),
        ),
        out_shape=jax.ShapeDtypeStruct((3, depth, n * width), BF16),
        cost_estimate=pl.CostEstimate(
            flops=0, bytes_accessed=12 * n * depth * width, transcendentals=0
        ),
    )(expert.astype(jnp.int32).reshape(1), *pieces)


def part_kernel(n, order_ref, mine_x_ref, other_x_ref, w_ref, *out_refs):
    width = w_ref.shape[2]
    first = order_ref[1] == 0
    mine, other = mine_x_ref[0], other_x_ref[0]
    x, dy = jnp.where(first, mine, other), jnp.where(first, other, mine)

    def fill(outs):
        for a, rows in enumerate((x, x, dy)):
            s = slice(a * width, (a + 1) * width)
            product = jnp.dot(rows, w_ref[a], preferred_element_type=F32).astype(BF16)
            lower = 0
            for out in outs:
                out[:, s] = product[lower : lower + out.shape[0]]
                lower += out.shape[0]

    if n == 1:
        fill(out_refs)
        return
    for i, out in enumerate(out_refs):
        pl.when(pl.program_id(0) == i)(functools.partial(fill, (out,)))


def stepper(steps, ring):
    if len(steps) > 2:
        return lambda i, o: (o[0] + (steps[0] - (i >> 1)) * (1 - 2 * (i & 1))) & (ring - 1)
    first, jump = steps[0], steps[-1] - steps[0]
    return lambda i, o: (o[0] + first + jump * i) & (ring - 1)


def parts(where, steps, mine, other, w, heights=None):
    ring, height, depth = mine.shape
    width = w.shape[2]
    n = len(steps)
    chunk = stepper(steps, ring)
    heights = heights or (height,) * n
    return call(
        functools.partial(part_kernel, n),
        grid_spec=pltpu.PrefetchScalarGridSpec(
            num_scalar_prefetch=1,
            grid=(n,),
            in_specs=[
                pl.BlockSpec((1, height, depth), lambda i, o: (chunk(i, o), 0, 0)),
                pl.BlockSpec((1, height, depth), lambda i, o: (chunk(i, o), 0, 0)),
                pl.BlockSpec(w.shape, lambda i, o: (0, 0, 0)),
            ],
            out_specs=[pl.BlockSpec((h, 3 * width), lambda i, o: (0, 0)) for h in heights],
        ),
        out_shape=[jax.ShapeDtypeStruct((h, 3 * width), BF16) for h in heights],
        cost_estimate=pl.CostEstimate(
            flops=n * height * depth * width * 6,
            bytes_accessed=2 * (n * height * (2 * depth + 3 * width) + 3 * depth * width),
            transcendentals=0,
        ),
    )(where, mine, other, w)


def merge_kernel(lower, own_ref, got_ref, out_ref):
    upper = lower + got_ref.shape[0]
    if lower:
        out_ref[:lower] = own_ref[:lower]
    if upper < out_ref.shape[0]:
        out_ref[upper:] = own_ref[upper:]
    out_ref[lower:upper] = own_ref[lower:upper] + got_ref[...]


def merge(own, got, lower):
    return call(
        functools.partial(merge_kernel, lower),
        out_shape=jax.ShapeDtypeStruct(own.shape, BF16),
        cost_estimate=pl.CostEstimate(
            flops=own.size, bytes_accessed=6 * own.size, transcendentals=0
        ),
    )(own, got)


def act_kernel(a_ref, b_ref, c_ref, out_ref):
    width = a_ref.shape[1] // 3

    def total(k):
        s = slice(k * width, (k + 1) * width)
        return a_ref[:, s].astype(F32) + b_ref[:, s].astype(F32) + c_ref[:, s].astype(F32)

    gate, up, back = total(0), total(1), total(2)
    sig = jax.nn.sigmoid(gate)
    silu = gate * sig
    out_ref[:, :width] = (back * up * sig * (1.0 + gate * (1.0 - sig))).astype(BF16)
    out_ref[:, width : 2 * width] = (back * silu).astype(BF16)
    out_ref[:, 2 * width :] = (silu * up).astype(BF16)


def contract_last(left, right):
    return lax.dot_general(
        left, right, (((1,), (1,)), ((), ())), preferred_element_type=F32
    )


def back_rows(acts, first, w_ref, keep_ref, send_ref, all_ref, lower, upper):
    width = w_ref.shape[2]
    d_gate, d_up, hidden = (acts[:, k * width : (k + 1) * width] for k in range(3))
    out = contract_last(hidden, w_ref[2])
    d_x = contract_last(d_gate, w_ref[0]) + contract_last(d_up, w_ref[1])
    keep_ref[0, lower:upper] = jnp.where(first, out, d_x).astype(BF16)
    send_ref[0, lower:upper] = jnp.where(first, d_x, out).astype(BF16)
    all_ref[0, lower:upper] = acts


def back_kernel(n, halves, order_ref, *refs):
    chunks, w_ref = refs[:n], refs[n]
    outs = refs[-3:]
    first = order_ref[1] == 0
    if halves:
        lower = 0
        for c in chunks:
            back_rows(c[...], first, w_ref, *outs, lower, lower + c.shape[0])
            lower += c.shape[0]
        return
    for i, c in enumerate(chunks):

        @pl.when(pl.program_id(0) == i)
        def _():
            back_rows(c[...], first, w_ref, *outs, 0, c.shape[0])


def back(where, steps, chunks, w, held, n_chunks, halves=False):
    n = len(chunks)
    chunk = stepper(steps, n_chunks)
    height = sum(c.shape[0] for c in chunks) if halves else chunks[0].shape[0]
    width3 = chunks[0].shape[1]
    depth = w.shape[1]
    grid = len(steps)
    in_specs = [pl.BlockSpec(c.shape, lambda i, o: (0, 0)) for c in chunks]
    in_specs.append(pl.BlockSpec(w.shape, lambda i, o: (0, 0, 0)))
    aliases = {}
    extra = held or ()
    if halves:
        extra = held[2:]
    if extra:
        in_specs += [pl.BlockSpec(memory_space=pl.ANY)] * len(extra)
        aliases = {n + 2 + i: 3 - len(extra) + i for i in range(len(extra))}

    def sums(i, o):
        return (0 if halves else chunk(i, o), 0, 0)

    n_sums = 1 if halves else n_chunks
    return call(
        functools.partial(back_kernel, n, halves),
        grid_spec=pltpu.PrefetchScalarGridSpec(
            num_scalar_prefetch=1,
            grid=(grid,),
            in_specs=in_specs,
            out_specs=[
                pl.BlockSpec((1, height, depth), sums),
                pl.BlockSpec((1, height, depth), sums),
                pl.BlockSpec((1, height, width3), lambda i, o: (chunk(i, o), 0, 0)),
            ],
        ),
        out_shape=[
            jax.ShapeDtypeStruct((n_sums, height, depth), BF16),
            jax.ShapeDtypeStruct((n_sums, height, depth), BF16),
            jax.ShapeDtypeStruct((n_chunks, height, width3), BF16),
        ],
        input_output_aliases=aliases,
        cost_estimate=pl.CostEstimate(
            flops=grid * height * depth * width3 * 2,
            bytes_accessed=2 * (grid * height * (2 * width3 + 2 * depth) + depth * width3),
            transcendentals=0,
        ),
    )(where, *chunks, w, *extra)


def join_kernel(keep_ref, got_ref, out_ref):
    out_ref[...] = (keep_ref[...].astype(F32) + got_ref[...].astype(F32)).astype(BF16)


def join_last_kernel(where_ref, keep_ref, got_ref, held_ref, out_ref):
    join_kernel(keep_ref, got_ref, out_ref)


def join(keep, got):
    shape = keep.shape
    block = pl.BlockSpec((shape[0] // 2, *shape[1:]), lambda i: (i, 0, 0))
    return call(
        join_kernel,
        grid=(2,),
        in_specs=[block, block],
        out_specs=block,
        out_shape=jax.ShapeDtypeStruct(shape, BF16),
    )(keep, got)


def join_last(where, steps, keep, got, held):
    shape = keep.shape
    chunk = stepper(steps, held.shape[0])
    flat = pl.BlockSpec(shape, lambda i, o: (0, 0, 0))
    return call(
        join_last_kernel,
        grid_spec=pltpu.PrefetchScalarGridSpec(
            num_scalar_prefetch=1,
            grid=(1,),
            in_specs=[flat, flat, pl.BlockSpec(memory_space=pl.ANY)],
            out_specs=pl.BlockSpec(shape, lambda i, o: (chunk(i, o), 0, 0)),
        ),
        out_shape=jax.ShapeDtypeStruct(held.shape, BF16),
        input_output_aliases={3: 0},
    )(where, keep, got, held)


def split_kernel(sums_ref, out_ref):
    slots = out_ref.shape[1]
    total = sum(sums_ref[k].astype(F32) for k in range(sums_ref.shape[0])).astype(BF16)
    for k in range(out_ref.shape[0]):
        out_ref[k] = total[k * slots : (k + 1) * slots]


def contract_rows(left, right):
    return lax.dot_general(
        left, right, (((0,), (0,)), ((), ())), preferred_element_type=F32
    )


def step(tokens, route_ids, route_gates, d_out, gate_saved, up_saved, down_saved):
    experts = lax.axis_size("expert")
    ring = lax.axis_size("tensor")
    n_chips = lax.axis_size("ylo") * lax.axis_size("x")
    tok_count, depth = tokens.shape
    slots = 5 * tok_count // 8
    part = gate_saved.shape[2]
    width = experts * part
    core = lax.axis_index("core")

    ids_row, gates_row = route_ids.T, route_gates.T
    lows = lax.axis_size("ylo")
    sent = pl.pallas_call(
        send_kernel,
        out_shape=jax.ShapeDtypeStruct((lows, 2 * experts, slots, depth), BF16),
    )(ids_row, gates_row, tokens, d_out)
    height = 2 * experts * slots
    own = lax.all_to_all(
        sent.reshape(lows * 2 * experts, slots, depth), NEAR, 0, 0, tiled=True
    ).reshape(lows * height, depth)
    expert = lax.axis_index("expert")
    pieces = pack(expert, (gate_saved, up_saved, down_saved))
    pieces = [pieces[0]] + [
        lax.ppermute(pieces[r], "expert", [(i, (i + r) % experts) for i in range(experts)])
        for r in range(1, experts)
    ]
    w = place(expert, pieces)
    mine = lax.all_to_all(
        jnp.broadcast_to(own[None], (n_chips // lows, lows * height, depth)), "x", 0, 0, tiled=True
    ).reshape(n_chips, height, depth)
    swap = [(0, 1), (1, 0)]
    other = lax.ppermute(mine, "core", swap)

    right = [(i, (i + 1) % ring) for i in range(ring)]
    left = [(i, (i - 1) % ring) for i in range(ring)]
    here = lax.axis_index("tensor")

    def both(to_right, to_left):
        return (lax.ppermute(to_right, "tensor", right), lax.ppermute(to_left, "tensor", left))

    where = jnp.stack([here, core]).astype(jnp.int32)

    half = height // 16 * 8
    far = parts(where, (4,), mine, other, w, (half, height - half))
    got = both(*far)
    near = parts(where, (3, -3), mine, other, w)
    to_right = merge(near[0], got[0], 0)
    to_left = merge(near[1], got[1], half)
    got = both(to_right, to_left)
    near = parts(where, (2, -2, 1, -1, 0), mine, other, w)
    got = both(got[0] + near[0], got[1] + near[1])
    got = both(got[0] + near[2], got[1] + near[3])
    acts = call(
        act_kernel, out_shape=jax.ShapeDtypeStruct((height, 3 * width), BF16)
    )(near[4], *got)

    got = both(acts, acts)
    held = back(where, (0,), (acts,), w, None, ring)
    for k in (1, 2, 3):
        now = got
        if k < 3:
            got = both(*now)
        else:
            got = both(now[0][:half], now[1][half:])
        held = back(where, (-k, k,), now, w, held, ring)
    early = lax.ppermute(held[1], "core", swap)
    keep, send, acts = back(where, (4,), got, w, held, ring, halves=True)
    late = lax.ppermute(send, "core", swap)
    sums = join(held[0], early)
    sums = join_last(where, (4,), keep, late, sums)
    sums = lax.all_to_all(sums, ("x", "ylo"), 0, 0, tiled=True)
    own = call(
        split_kernel,
        out_shape=jax.ShapeDtypeStruct((2 * experts, slots, depth), BF16),
    )(sums)
    returned = lax.all_to_all(own, ("core", "expert"), 0, 0, tiled=True)
    out, d_tokens = call(
        finish_kernel,
        out_shape=[jax.ShapeDtypeStruct(tokens.shape, BF16)] * 2,
    )(ids_row, gates_row, returned)

    acts = acts.reshape(ring * height, 3 * width)
    x = jnp.where(core == 0, mine, other).reshape(n_chips * height, depth)
    dy = jnp.where(core == 0, other, mine).reshape(n_chips * height, depth)
    grads = [
        contract_rows(x if a < 2 else dy, acts[:, a * width : (a + 1) * width]).astype(BF16)[None]
        for a in range(3)
    ]
    return (out, d_tokens, *grads)


def solution(mesh):
    fine = Mesh(
        mesh.devices.reshape(2, 4, 2, 4, 8), ("ylo", "x", "core", "expert", "tensor")
    )
    dp = ("ylo", "x", "core")
    tok = P((*dp, "expert"), "tensor")
    route = P((*dp, "expert"), None)
    saved = P(None, "tensor", (*dp, "expert"))
    grad = P("expert", "tensor", dp)
    return jax.shard_map(
        step,
        mesh=fine,
        in_specs=(tok, route, route, tok, saved, saved, saved),
        out_specs=(tok, tok, grad, grad, grad),
        check_vma=False,
    )
```

```python
import functools

import jax
import jax.numpy as jnp
from jax import lax
from jax.experimental import pallas as pl
from jax.experimental.pallas import tpu as pltpu
from jax.sharding import Mesh, PartitionSpec as P


NEAR = ("ylo", "core", "expert")
BF16 = jnp.bfloat16
F32 = jnp.float32
call = functools.partial(
    pl.pallas_call, compiler_params=pltpu.CompilerParams(vmem_limit_bytes=14 << 20)
)


def place_of(ids_row, expert, slots):
    tokens = ids_row.shape[1]
    hits = jnp.sum((ids_row == expert).astype(F32), axis=0, keepdims=True)
    earlier = (
        lax.broadcasted_iota(jnp.int32, (tokens, tokens), 0)
        < lax.broadcasted_iota(jnp.int32, (tokens, tokens), 1)
    ).astype(F32)
    before = jnp.dot(
        jnp.broadcast_to(hits, (8, tokens)), earlier, preferred_element_type=F32
    )[:1].astype(jnp.int32)
    slot = lax.broadcasted_iota(jnp.int32, (slots, tokens), 0)
    return jnp.where((slot == before) & (hits > 0.5), 1.0, 0.0).astype(F32)


def send_kernel(ids_ref, gates_ref, tok_ref, dout_ref, out_ref):
    copies, both, slots, _ = out_ref.shape
    experts = both // 2
    ids, gates = ids_ref[...], gates_ref[...]
    for e in range(experts):
        place = place_of(ids, e, slots)
        gate_row = jnp.sum(jnp.where(ids == e, gates, 0.0), axis=0, keepdims=True)
        gate_slot = jnp.sum(place * gate_row, axis=1, keepdims=True)
        pick = place.astype(BF16)
        rows = jnp.dot(pick, tok_ref[...], preferred_element_type=F32).astype(BF16)
        grads = jnp.dot(pick, dout_ref[...], preferred_element_type=F32)
        grads = (gate_slot * grads).astype(BF16)
        for c in range(copies):
            out_ref[c, e] = rows
            out_ref[c, experts + e] = grads


def finish_kernel(ids_ref, gates_ref, back_ref, out_ref, dtok_ref):
    experts, slots = back_ref.shape[0] // 2, back_ref.shape[1]
    ids, gates = ids_ref[...], gates_ref[...]
    tokens = ids.shape[1]
    eye = lax.broadcasted_iota(jnp.int32, (tokens, tokens), 0) == lax.broadcasted_iota(
        jnp.int32, (tokens, tokens), 1
    )
    out = jnp.zeros(out_ref.shape, F32)
    dtok = jnp.zeros(dtok_ref.shape, F32)
    for e in range(experts):
        pick = place_of(ids, e, slots).astype(BF16)
        gate_row = jnp.sum(jnp.where(ids == e, gates, 0.0), axis=0, keepdims=True)
        gate_col = jnp.sum(jnp.where(eye, gate_row, 0.0), axis=1, keepdims=True)
        spread = functools.partial(
            lax.dot_general,
            pick,
            dimension_numbers=(((0,), (0,)), ((), ())),
            preferred_element_type=F32,
        )
        out += gate_col * spread(back_ref[e])
        dtok += spread(back_ref[experts + e])
    out_ref[...] = out.astype(BF16)
    dtok_ref[...] = dtok.astype(BF16)


def pack_kernel(expert_ref, *refs):
    saved, outs = refs[:3], refs[3:]
    width = saved[0].shape[2]
    for r, out in enumerate(outs):

        @pl.when(pl.program_id(0) == r)
        def _():
            for a in range(3):
                out[:, a * width : (a + 1) * width] = saved[a][0]


def pack(expert, saved):
    n, depth, width = saved[0].shape
    return call(
        pack_kernel,
        grid_spec=pltpu.PrefetchScalarGridSpec(
            num_scalar_prefetch=1,
            grid=(n,),
            in_specs=[pl.BlockSpec((1, depth, width), lambda i, e: ((e[0] + i) & (n - 1), 0, 0))] * 3,
            out_specs=[pl.BlockSpec((depth, 3 * width), lambda i, e: (0, 0))] * n,
        ),
        out_shape=[jax.ShapeDtypeStruct((depth, 3 * width), BF16)] * n,
        cost_estimate=pl.CostEstimate(
            flops=0, bytes_accessed=12 * n * depth * width, transcendentals=0
        ),
    )(expert.astype(jnp.int32).reshape(1), *saved)


def place_kernel(expert_ref, *refs):
    pieces, out = refs[:-1], refs[-1]
    width = out.shape[2]
    for r, piece in enumerate(pieces):

        @pl.when(pl.program_id(0) == r)
        def _():
            for a in range(3):
                out[a] = piece[:, a * width : (a + 1) * width]


def place(expert, pieces):
    n, (depth, width3) = len(pieces), pieces[0].shape
    width = width3 // 3
    return call(
        place_kernel,
        grid_spec=pltpu.PrefetchScalarGridSpec(
            num_scalar_prefetch=1,
            grid=(n,),
            in_specs=[pl.BlockSpec((depth, width3), lambda i, e: (0, 0))] * n,
            out_specs=pl.BlockSpec((3, depth, width), lambda i, e: (0, 0, (e[0] - i) & (n - 1))),
        ),
        out_shape=jax.ShapeDtypeStruct((3, depth, n * width), BF16),
        cost_estimate=pl.CostEstimate(
            flops=0, bytes_accessed=12 * n * depth * width, transcendentals=0
        ),
    )(expert.astype(jnp.int32).reshape(1), *pieces)


def part_kernel(n, order_ref, mine_x_ref, other_x_ref, w_ref, *out_refs):
    width = w_ref.shape[2]
    first = order_ref[1] == 0
    mine, other = mine_x_ref[0], other_x_ref[0]
    x, dy = jnp.where(first, mine, other), jnp.where(first, other, mine)

    def fill(outs):
        for a, rows in enumerate((x, x, dy)):
            s = slice(a * width, (a + 1) * width)
            product = jnp.dot(rows, w_ref[a], preferred_element_type=F32).astype(BF16)
            lower = 0
            for out in outs:
                out[:, s] = product[lower : lower + out.shape[0]]
                lower += out.shape[0]

    if n == 1:
        fill(out_refs)
        return
    for i, out in enumerate(out_refs):
        pl.when(pl.program_id(0) == i)(functools.partial(fill, (out,)))


def stepper(steps, ring):
    if len(steps) > 2:
        return lambda i, o: (o[0] + (steps[0] - (i >> 1)) * (1 - 2 * (i & 1))) & (ring - 1)
    first, jump = steps[0], steps[-1] - steps[0]
    return lambda i, o: (o[0] + first + jump * i) & (ring - 1)


def parts(where, steps, mine, other, w, heights=None):
    ring, height, depth = mine.shape
    width = w.shape[2]
    n = len(steps)
    chunk = stepper(steps, ring)
    heights = heights or (height,) * n
    return call(
        functools.partial(part_kernel, n),
        grid_spec=pltpu.PrefetchScalarGridSpec(
            num_scalar_prefetch=1,
            grid=(n,),
            in_specs=[
                pl.BlockSpec((1, height, depth), lambda i, o: (chunk(i, o), 0, 0)),
                pl.BlockSpec((1, height, depth), lambda i, o: (chunk(i, o), 0, 0)),
                pl.BlockSpec(w.shape, lambda i, o: (0, 0, 0)),
            ],
            out_specs=[pl.BlockSpec((h, 3 * width), lambda i, o: (0, 0)) for h in heights],
        ),
        out_shape=[jax.ShapeDtypeStruct((h, 3 * width), BF16) for h in heights],
        cost_estimate=pl.CostEstimate(
            flops=n * height * depth * width * 6,
            bytes_accessed=2 * (n * height * (2 * depth + 3 * width) + 3 * depth * width),
            transcendentals=0,
        ),
    )(where, mine, other, w)


def merge_kernel(lower, own_ref, got_ref, out_ref):
    upper = lower + got_ref.shape[0]
    if lower:
        out_ref[:lower] = own_ref[:lower]
    if upper < out_ref.shape[0]:
        out_ref[upper:] = own_ref[upper:]
    out_ref[lower:upper] = own_ref[lower:upper] + got_ref[...]


def merge(own, got, lower):
    return call(
        functools.partial(merge_kernel, lower),
        out_shape=jax.ShapeDtypeStruct(own.shape, BF16),
        cost_estimate=pl.CostEstimate(
            flops=own.size, bytes_accessed=6 * own.size, transcendentals=0
        ),
    )(own, got)


def act_kernel(a_ref, b_ref, c_ref, out_ref):
    width = a_ref.shape[1] // 3

    def total(k):
        s = slice(k * width, (k + 1) * width)
        return a_ref[:, s].astype(F32) + b_ref[:, s].astype(F32) + c_ref[:, s].astype(F32)

    gate, up, back = total(0), total(1), total(2)
    sig = jax.nn.sigmoid(gate)
    silu = gate * sig
    out_ref[:, :width] = (back * up * sig * (1.0 + gate * (1.0 - sig))).astype(BF16)
    out_ref[:, width : 2 * width] = (back * silu).astype(BF16)
    out_ref[:, 2 * width :] = (silu * up).astype(BF16)


def contract_last(left, right):
    return lax.dot_general(
        left, right, (((1,), (1,)), ((), ())), preferred_element_type=F32
    )


def back_rows(acts, first, w_ref, keep_ref, send_ref, all_ref, lower, upper):
    width = w_ref.shape[2]
    d_gate, d_up, hidden = (acts[:, k * width : (k + 1) * width] for k in range(3))
    out = contract_last(hidden, w_ref[2])
    d_x = contract_last(d_gate, w_ref[0]) + contract_last(d_up, w_ref[1])
    keep_ref[0, lower:upper] = jnp.where(first, out, d_x).astype(BF16)
    send_ref[0, lower:upper] = jnp.where(first, d_x, out).astype(BF16)
    all_ref[0, lower:upper] = acts


def back_kernel(n, halves, order_ref, *refs):
    chunks, w_ref = refs[:n], refs[n]
    outs = refs[-3:]
    first = order_ref[1] == 0
    if halves:
        lower = 0
        for c in chunks:
            back_rows(c[...], first, w_ref, *outs, lower, lower + c.shape[0])
            lower += c.shape[0]
        return
    for i, c in enumerate(chunks):

        @pl.when(pl.program_id(0) == i)
        def _():
            back_rows(c[...], first, w_ref, *outs, 0, c.shape[0])


def back(where, steps, chunks, w, held, n_chunks, halves=False):
    n = len(chunks)
    chunk = stepper(steps, n_chunks)
    height = sum(c.shape[0] for c in chunks) if halves else chunks[0].shape[0]
    width3 = chunks[0].shape[1]
    depth = w.shape[1]
    grid = len(steps)
    in_specs = [pl.BlockSpec(c.shape, lambda i, o: (0, 0)) for c in chunks]
    in_specs.append(pl.BlockSpec(w.shape, lambda i, o: (0, 0, 0)))
    aliases = {}
    extra = held or ()
    if halves:
        extra = held[2:]
    if extra:
        in_specs += [pl.BlockSpec(memory_space=pl.ANY)] * len(extra)
        aliases = {n + 2 + i: 3 - len(extra) + i for i in range(len(extra))}

    def sums(i, o):
        return (0 if halves else chunk(i, o), 0, 0)

    n_sums = 1 if halves else n_chunks
    return call(
        functools.partial(back_kernel, n, halves),
        grid_spec=pltpu.PrefetchScalarGridSpec(
            num_scalar_prefetch=1,
            grid=(grid,),
            in_specs=in_specs,
            out_specs=[
                pl.BlockSpec((1, height, depth), sums),
                pl.BlockSpec((1, height, depth), sums),
                pl.BlockSpec((1, height, width3), lambda i, o: (chunk(i, o), 0, 0)),
            ],
        ),
        out_shape=[
            jax.ShapeDtypeStruct((n_sums, height, depth), BF16),
            jax.ShapeDtypeStruct((n_sums, height, depth), BF16),
            jax.ShapeDtypeStruct((n_chunks, height, width3), BF16),
        ],
        input_output_aliases=aliases,
        cost_estimate=pl.CostEstimate(
            flops=grid * height * depth * width3 * 2,
            bytes_accessed=2 * (grid * height * (2 * width3 + 2 * depth) + depth * width3),
            transcendentals=0,
        ),
    )(where, *chunks, w, *extra)


def join_kernel(where_ref, keep_ref, got_ref, last_keep_ref, last_got_ref, out_ref):
    out_ref[...] = (keep_ref[...].astype(F32) + got_ref[...].astype(F32)).astype(BF16)
    ring = 2 * pl.num_programs(0)
    last = (where_ref[0] + 4) & (ring - 1)

    @pl.when(pl.program_id(0) == last >> 1)
    def _():
        total = last_keep_ref[...].astype(F32) + last_got_ref[...].astype(F32)
        out_ref[pl.ds(last & 1, 1)] = total.astype(BF16)


def join(where, keep, got, last_keep, last_got):
    n, height, depth = keep.shape
    pair = pl.BlockSpec((2, height, depth), lambda i, o: (i, 0, 0))
    one = pl.BlockSpec((1, height, depth), lambda i, o: (0, 0, 0))
    return call(
        join_kernel,
        grid_spec=pltpu.PrefetchScalarGridSpec(
            num_scalar_prefetch=1,
            grid=(n // 2,),
            in_specs=[pair, pair, one, one],
            out_specs=pair,
        ),
        out_shape=pltpu.HBM(keep.shape, BF16),
    )(where, keep, got, last_keep, last_got)


def split_kernel(sums_ref, out_ref):
    slots = out_ref.shape[1]
    total = sum(sums_ref[k].astype(F32) for k in range(sums_ref.shape[0])).astype(BF16)
    for k in range(out_ref.shape[0]):
        out_ref[k] = total[k * slots : (k + 1) * slots]


def contract_rows(left, right):
    return lax.dot_general(
        left, right, (((0,), (0,)), ((), ())), preferred_element_type=F32
    )


def step(tokens, route_ids, route_gates, d_out, gate_saved, up_saved, down_saved):
    experts = lax.axis_size("expert")
    ring = lax.axis_size("tensor")
    n_chips = lax.axis_size("ylo") * lax.axis_size("x")
    tok_count, depth = tokens.shape
    slots = 5 * tok_count // 8
    part = gate_saved.shape[2]
    width = experts * part
    core = lax.axis_index("core")

    ids_row, gates_row = route_ids.T, route_gates.T
    lows = lax.axis_size("ylo")
    sent = pl.pallas_call(
        send_kernel,
        out_shape=jax.ShapeDtypeStruct((lows, 2 * experts, slots, depth), BF16),
    )(ids_row, gates_row, tokens, d_out)
    height = 2 * experts * slots
    own = lax.all_to_all(
        sent.reshape(lows * 2 * experts, slots, depth), NEAR, 0, 0, tiled=True
    ).reshape(lows * height, depth)
    expert = lax.axis_index("expert")
    pieces = pack(expert, (gate_saved, up_saved, down_saved))
    pieces = [pieces[0]] + [
        lax.ppermute(pieces[r], "expert", [(i, (i + r) % experts) for i in range(experts)])
        for r in range(1, experts)
    ]
    w = place(expert, pieces)
    mine = lax.all_to_all(
        jnp.broadcast_to(own[None], (n_chips // lows, lows * height, depth)), "x", 0, 0, tiled=True
    ).reshape(n_chips, height, depth)
    swap = [(0, 1), (1, 0)]
    other = lax.ppermute(mine, "core", swap)

    right = [(i, (i + 1) % ring) for i in range(ring)]
    left = [(i, (i - 1) % ring) for i in range(ring)]
    here = lax.axis_index("tensor")

    def both(to_right, to_left):
        return (lax.ppermute(to_right, "tensor", right), lax.ppermute(to_left, "tensor", left))

    where = jnp.stack([here, core]).astype(jnp.int32)

    half = height // 22 * 8
    far = parts(where, (4,), mine, other, w, (half, height - half))
    got = both(*far)
    near = parts(where, (3, -3), mine, other, w)
    to_right = merge(near[0], got[0], 0)
    to_left = merge(near[1], got[1], half)
    got = both(to_right, to_left)
    near = parts(where, (2, -2, 1, -1, 0), mine, other, w)
    got = both(got[0] + near[0], got[1] + near[1])
    got = both(got[0] + near[2], got[1] + near[3])
    acts = call(
        act_kernel, out_shape=jax.ShapeDtypeStruct((height, 3 * width), BF16)
    )(near[4], *got)

    got = both(acts, acts)
    held = back(where, (0,), (acts,), w, None, ring)
    for k in (1, 2, 3):
        now = got
        if k < 3:
            got = both(*now)
        else:
            got = both(now[0][:half], now[1][half:])
        held = back(where, (-k, k,), now, w, held, ring)
    early = lax.ppermute(held[1], "core", swap)
    keep, send, acts = back(where, (4,), got, w, held, ring, halves=True)
    late = lax.ppermute(send, "core", swap)
    sums = join(where, held[0], early, keep, late)
    sums = lax.all_to_all(sums, ("x", "ylo"), 0, 0, tiled=True)
    own = call(
        split_kernel,
        out_shape=jax.ShapeDtypeStruct((2 * experts, slots, depth), BF16),
    )(sums)
    returned = lax.all_to_all(own, ("core", "expert"), 0, 0, tiled=True)
    out, d_tokens = call(
        finish_kernel,
        out_shape=[jax.ShapeDtypeStruct(tokens.shape, BF16)] * 2,
    )(ids_row, gates_row, returned)

    acts = acts.reshape(ring * height, 3 * width)
    x = jnp.where(core == 0, mine, other).reshape(n_chips * height, depth)
    dy = jnp.where(core == 0, other, mine).reshape(n_chips * height, depth)
    grads = [
        contract_rows(x if a < 2 else dy, acts[:, a * width : (a + 1) * width]).astype(BF16)[None]
        for a in range(3)
    ]
    return (out, d_tokens, *grads)


def solution(mesh):
    fine = Mesh(
        mesh.devices.reshape(2, 4, 2, 4, 8), ("ylo", "x", "core", "expert", "tensor")
    )
    dp = ("ylo", "x", "core")
    tok = P((*dp, "expert"), "tensor")
    route = P((*dp, "expert"), None)
    saved = P(None, "tensor", (*dp, "expert"))
    grad = P("expert", "tensor", dp)
    return jax.shard_map(
        step,
        mesh=fine,
        in_specs=(tok, route, route, tok, saved, saved, saved),
        out_specs=(tok, tok, grad, grad, grad),
        check_vma=False,
    )
```

```python
import functools

import jax
import jax.numpy as jnp
from jax import lax
from jax.experimental import pallas as pl
from jax.experimental.pallas import tpu as pltpu
from jax.sharding import Mesh, PartitionSpec as P


NEAR = ("ylo", "core", "expert")
BF16 = jnp.bfloat16
F32 = jnp.float32
call = functools.partial(
    pl.pallas_call, compiler_params=pltpu.CompilerParams(vmem_limit_bytes=14 << 20)
)


def place_of(ids_row, expert, slots):
    tokens = ids_row.shape[1]
    hits = jnp.sum((ids_row == expert).astype(F32), axis=0, keepdims=True)
    earlier = (
        lax.broadcasted_iota(jnp.int32, (tokens, tokens), 0)
        < lax.broadcasted_iota(jnp.int32, (tokens, tokens), 1)
    ).astype(F32)
    before = jnp.dot(
        jnp.broadcast_to(hits, (8, tokens)), earlier, preferred_element_type=F32
    )[:1].astype(jnp.int32)
    slot = lax.broadcasted_iota(jnp.int32, (slots, tokens), 0)
    return jnp.where((slot == before) & (hits > 0.5), 1.0, 0.0).astype(F32)


def send_kernel(ids_ref, gates_ref, tok_ref, dout_ref, out_ref):
    copies, both, slots, _ = out_ref.shape
    experts = both // 2
    ids, gates = ids_ref[...], gates_ref[...]
    for e in range(experts):
        place = place_of(ids, e, slots)
        gate_row = jnp.sum(jnp.where(ids == e, gates, 0.0), axis=0, keepdims=True)
        gate_slot = jnp.sum(place * gate_row, axis=1, keepdims=True)
        pick = place.astype(BF16)
        rows = jnp.dot(pick, tok_ref[...], preferred_element_type=F32).astype(BF16)
        grads = jnp.dot(pick, dout_ref[...], preferred_element_type=F32)
        grads = (gate_slot * grads).astype(BF16)
        for c in range(copies):
            out_ref[c, e] = rows
            out_ref[c, experts + e] = grads


def finish_kernel(ids_ref, gates_ref, back_ref, out_ref, dtok_ref):
    experts, slots = back_ref.shape[0] // 2, back_ref.shape[1]
    ids, gates = ids_ref[...], gates_ref[...]
    tokens = ids.shape[1]
    eye = lax.broadcasted_iota(jnp.int32, (tokens, tokens), 0) == lax.broadcasted_iota(
        jnp.int32, (tokens, tokens), 1
    )
    out = jnp.zeros(out_ref.shape, F32)
    dtok = jnp.zeros(dtok_ref.shape, F32)
    for e in range(experts):
        pick = place_of(ids, e, slots).astype(BF16)
        gate_row = jnp.sum(jnp.where(ids == e, gates, 0.0), axis=0, keepdims=True)
        gate_col = jnp.sum(jnp.where(eye, gate_row, 0.0), axis=1, keepdims=True)
        spread = functools.partial(
            lax.dot_general,
            pick,
            dimension_numbers=(((0,), (0,)), ((), ())),
            preferred_element_type=F32,
        )
        out += gate_col * spread(back_ref[e])
        dtok += spread(back_ref[experts + e])
    out_ref[...] = out.astype(BF16)
    dtok_ref[...] = dtok.astype(BF16)


def pack_kernel(expert_ref, *refs):
    saved, outs = refs[:3], refs[3:]
    width = saved[0].shape[2]
    for r, out in enumerate(outs):

        @pl.when(pl.program_id(0) == r)
        def _():
            for a in range(3):
                out[:, a * width : (a + 1) * width] = saved[a][0]


def pack(expert, saved):
    n, depth, width = saved[0].shape
    return call(
        pack_kernel,
        grid_spec=pltpu.PrefetchScalarGridSpec(
            num_scalar_prefetch=1,
            grid=(n,),
            in_specs=[pl.BlockSpec((1, depth, width), lambda i, e: ((e[0] + i) & (n - 1), 0, 0))] * 3,
            out_specs=[pl.BlockSpec((depth, 3 * width), lambda i, e: (0, 0))] * n,
        ),
        out_shape=[jax.ShapeDtypeStruct((depth, 3 * width), BF16)] * n,
        cost_estimate=pl.CostEstimate(
            flops=0, bytes_accessed=12 * n * depth * width, transcendentals=0
        ),
    )(expert.astype(jnp.int32).reshape(1), *saved)


def place_kernel(expert_ref, *refs):
    pieces, out = refs[:2], refs[-1]
    width = out.shape[2]
    for i, piece in enumerate(pieces):

        @pl.when(pl.program_id(0) == i)
        def _():
            for a in range(3):
                out[a] = piece[:, a * width : (a + 1) * width]


def place(expert, first, pieces, n, held):
    depth, width3 = pieces[0].shape
    width = width3 // 3
    whole = pl.BlockSpec((depth, width3), lambda i, e: (0, 0))
    return call(
        place_kernel,
        grid_spec=pltpu.PrefetchScalarGridSpec(
            num_scalar_prefetch=1,
            grid=(2,),
            in_specs=[whole, whole] + [pl.BlockSpec(memory_space=pl.ANY)] * len(held),
            out_specs=pl.BlockSpec(
                (3, depth, width), lambda i, e: (0, 0, (e[0] - first - 2 * i) & (n - 1))
            ),
        ),
        out_shape=jax.ShapeDtypeStruct((3, depth, n * width), BF16),
        input_output_aliases={3: 0} if held else {},
        cost_estimate=pl.CostEstimate(
            flops=0, bytes_accessed=24 * depth * width, transcendentals=0
        ),
    )(expert.astype(jnp.int32).reshape(1), *pieces, *held)


def part_kernel(n, order_ref, mine_x_ref, other_x_ref, w_ref, *out_refs):
    width = w_ref.shape[2]
    first = order_ref[1] == 0
    mine, other = mine_x_ref[0], other_x_ref[0]
    x, dy = jnp.where(first, mine, other), jnp.where(first, other, mine)

    def fill(outs):
        for a, rows in enumerate((x, x, dy)):
            s = slice(a * width, (a + 1) * width)
            product = jnp.dot(rows, w_ref[a], preferred_element_type=F32).astype(BF16)
            lower = 0
            for out in outs:
                out[:, s] = product[lower : lower + out.shape[0]]
                lower += out.shape[0]

    if n == 1:
        fill(out_refs)
        return
    for i, out in enumerate(out_refs):
        pl.when(pl.program_id(0) == i)(functools.partial(fill, (out,)))


def stepper(steps, ring):
    if len(steps) > 2:
        return lambda i, o: (o[0] + (steps[0] - (i >> 1)) * (1 - 2 * (i & 1))) & (ring - 1)
    first, jump = steps[0], steps[-1] - steps[0]
    return lambda i, o: (o[0] + first + jump * i) & (ring - 1)


def parts(where, steps, mine, other, w, heights=None):
    ring, height, depth = mine.shape
    width = w.shape[2]
    n = len(steps)
    chunk = stepper(steps, ring)
    heights = heights or (height,) * n
    return call(
        functools.partial(part_kernel, n),
        grid_spec=pltpu.PrefetchScalarGridSpec(
            num_scalar_prefetch=1,
            grid=(n,),
            in_specs=[
                pl.BlockSpec((1, height, depth), lambda i, o: (chunk(i, o), 0, 0)),
                pl.BlockSpec((1, height, depth), lambda i, o: (chunk(i, o), 0, 0)),
                pl.BlockSpec(w.shape, lambda i, o: (0, 0, 0)),
            ],
            out_specs=[pl.BlockSpec((h, 3 * width), lambda i, o: (0, 0)) for h in heights],
        ),
        out_shape=[jax.ShapeDtypeStruct((h, 3 * width), BF16) for h in heights],
        cost_estimate=pl.CostEstimate(
            flops=n * height * depth * width * 6,
            bytes_accessed=2 * (n * height * (2 * depth + 3 * width) + 3 * depth * width),
            transcendentals=0,
        ),
    )(where, mine, other, w)


def merge_kernel(lower, own_ref, got_ref, out_ref):
    upper = lower + got_ref.shape[0]
    if lower:
        out_ref[:lower] = own_ref[:lower]
    if upper < out_ref.shape[0]:
        out_ref[upper:] = own_ref[upper:]
    out_ref[lower:upper] = own_ref[lower:upper] + got_ref[...]


def merge(own, got, lower):
    return call(
        functools.partial(merge_kernel, lower),
        out_shape=jax.ShapeDtypeStruct(own.shape, BF16),
        cost_estimate=pl.CostEstimate(
            flops=own.size, bytes_accessed=6 * own.size, transcendentals=0
        ),
    )(own, got)


def act_kernel(a_ref, b_ref, c_ref, out_ref):
    width = a_ref.shape[1] // 3

    def total(k):
        s = slice(k * width, (k + 1) * width)
        return a_ref[:, s].astype(F32) + b_ref[:, s].astype(F32) + c_ref[:, s].astype(F32)

    gate, up, back = total(0), total(1), total(2)
    sig = jax.nn.sigmoid(gate)
    silu = gate * sig
    out_ref[:, :width] = (back * up * sig * (1.0 + gate * (1.0 - sig))).astype(BF16)
    out_ref[:, width : 2 * width] = (back * silu).astype(BF16)
    out_ref[:, 2 * width :] = (silu * up).astype(BF16)


def contract_last(left, right):
    return lax.dot_general(
        left, right, (((1,), (1,)), ((), ())), preferred_element_type=F32
    )


def back_rows(acts, first, w_ref, keep_ref, send_ref, all_ref, lower, upper):
    width = w_ref.shape[2]
    d_gate, d_up, hidden = (acts[:, k * width : (k + 1) * width] for k in range(3))
    out = contract_last(hidden, w_ref[2])
    d_x = contract_last(d_gate, w_ref[0]) + contract_last(d_up, w_ref[1])
    keep_ref[0, lower:upper] = jnp.where(first, out, d_x).astype(BF16)
    send_ref[0, lower:upper] = jnp.where(first, d_x, out).astype(BF16)
    all_ref[0, lower:upper] = acts


def back_kernel(n, halves, order_ref, *refs):
    chunks, w_ref = refs[:n], refs[n]
    outs = refs[-3:]
    first = order_ref[1] == 0
    if halves:
        lower = 0
        for c in chunks:
            back_rows(c[...], first, w_ref, *outs, lower, lower + c.shape[0])
            lower += c.shape[0]
        return
    for i, c in enumerate(chunks):

        @pl.when(pl.program_id(0) == i)
        def _():
            back_rows(c[...], first, w_ref, *outs, 0, c.shape[0])


def back(where, steps, chunks, w, held, n_chunks, halves=False):
    n = len(chunks)
    chunk = stepper(steps, n_chunks)
    height = sum(c.shape[0] for c in chunks) if halves else chunks[0].shape[0]
    width3 = chunks[0].shape[1]
    depth = w.shape[1]
    grid = len(steps)
    in_specs = [pl.BlockSpec(c.shape, lambda i, o: (0, 0)) for c in chunks]
    in_specs.append(pl.BlockSpec(w.shape, lambda i, o: (0, 0, 0)))
    aliases = {}
    extra = held or ()
    if halves:
        extra = held[2:]
    if extra:
        in_specs += [pl.BlockSpec(memory_space=pl.ANY)] * len(extra)
        aliases = {n + 2 + i: 3 - len(extra) + i for i in range(len(extra))}

    def sums(i, o):
        return (0 if halves else chunk(i, o), 0, 0)

    n_sums = 1 if halves else n_chunks
    return call(
        functools.partial(back_kernel, n, halves),
        grid_spec=pltpu.PrefetchScalarGridSpec(
            num_scalar_prefetch=1,
            grid=(grid,),
            in_specs=in_specs,
            out_specs=[
                pl.BlockSpec((1, height, depth), sums),
                pl.BlockSpec((1, height, depth), sums),
                pl.BlockSpec((1, height, width3), lambda i, o: (chunk(i, o), 0, 0)),
            ],
        ),
        out_shape=[
            jax.ShapeDtypeStruct((n_sums, height, depth), BF16),
            jax.ShapeDtypeStruct((n_sums, height, depth), BF16),
            jax.ShapeDtypeStruct((n_chunks, height, width3), BF16),
        ],
        input_output_aliases=aliases,
        cost_estimate=pl.CostEstimate(
            flops=grid * height * depth * width3 * 2,
            bytes_accessed=2 * (grid * height * (2 * width3 + 2 * depth) + depth * width3),
            transcendentals=0,
        ),
    )(where, *chunks, w, *extra)


def join_kernel(where_ref, keep_ref, got_ref, last_keep_ref, last_got_ref, out_ref):
    out_ref[...] = (keep_ref[...].astype(F32) + got_ref[...].astype(F32)).astype(BF16)
    ring = 2 * pl.num_programs(0)
    last = (where_ref[0] + 4) & (ring - 1)

    @pl.when(pl.program_id(0) == last >> 1)
    def _():
        total = last_keep_ref[...].astype(F32) + last_got_ref[...].astype(F32)
        out_ref[pl.ds(last & 1, 1)] = total.astype(BF16)


def join(where, keep, got, last_keep, last_got):
    n, height, depth = keep.shape
    pair = pl.BlockSpec((2, height, depth), lambda i, o: (i, 0, 0))
    one = pl.BlockSpec((1, height, depth), lambda i, o: (0, 0, 0))
    return call(
        join_kernel,
        grid_spec=pltpu.PrefetchScalarGridSpec(
            num_scalar_prefetch=1,
            grid=(n // 2,),
            in_specs=[pair, pair, one, one],
            out_specs=pair,
        ),
        out_shape=pltpu.HBM(keep.shape, BF16),
    )(where, keep, got, last_keep, last_got)


def split_kernel(sums_ref, out_ref):
    slots = out_ref.shape[1]
    total = sum(sums_ref[k].astype(F32) for k in range(sums_ref.shape[0])).astype(BF16)
    for k in range(out_ref.shape[0]):
        out_ref[k] = total[k * slots : (k + 1) * slots]


def contract_rows(left, right):
    return lax.dot_general(
        left, right, (((0,), (0,)), ((), ())), preferred_element_type=F32
    )


def step(tokens, route_ids, route_gates, d_out, gate_saved, up_saved, down_saved):
    experts = lax.axis_size("expert")
    ring = lax.axis_size("tensor")
    n_chips = lax.axis_size("ylo") * lax.axis_size("x")
    tok_count, depth = tokens.shape
    slots = 5 * tok_count // 8
    part = gate_saved.shape[2]
    width = experts * part
    core = lax.axis_index("core")

    ids_row, gates_row = route_ids.T, route_gates.T
    lows = lax.axis_size("ylo")
    sent = pl.pallas_call(
        send_kernel,
        out_shape=jax.ShapeDtypeStruct((lows, 2 * experts, slots, depth), BF16),
    )(ids_row, gates_row, tokens, d_out)
    height = 2 * experts * slots
    own = lax.all_to_all(
        sent.reshape(lows * 2 * experts, slots, depth), NEAR, 0, 0, tiled=True
    ).reshape(lows * height, depth)
    expert = lax.axis_index("expert")
    pieces = pack(expert, (gate_saved, up_saved, down_saved))
    pieces = [pieces[0]] + [
        lax.ppermute(pieces[r], "expert", [(i, (i + r) % experts) for i in range(experts)])
        for r in range(1, experts)
    ]
    w = place(expert, 0, pieces[0::2], experts, ())
    w = place(expert, 1, pieces[1::2], experts, (w,))
    mine = lax.all_to_all(
        jnp.broadcast_to(own[None], (n_chips // lows, lows * height, depth)), "x", 0, 0, tiled=True
    ).reshape(n_chips, height, depth)
    swap = [(0, 1), (1, 0)]
    other = lax.ppermute(mine, "core", swap)

    right = [(i, (i + 1) % ring) for i in range(ring)]
    left = [(i, (i - 1) % ring) for i in range(ring)]
    here = lax.axis_index("tensor")

    def both(to_right, to_left):
        return (lax.ppermute(to_right, "tensor", right), lax.ppermute(to_left, "tensor", left))

    where = jnp.stack([here, core]).astype(jnp.int32)

    half = height // 22 * 8
    far = parts(where, (4,), mine, other, w, (half, height - half))
    got = both(*far)
    near = parts(where, (3, -3), mine, other, w)
    to_right = merge(near[0], got[0], 0)
    to_left = merge(near[1], got[1], half)
    got = both(to_right, to_left)
    near = parts(where, (2, -2, 1, -1, 0), mine, other, w)
    got = both(got[0] + near[0], got[1] + near[1])
    got = both(got[0] + near[2], got[1] + near[3])
    acts = call(
        act_kernel, out_shape=jax.ShapeDtypeStruct((height, 3 * width), BF16)
    )(near[4], *got)

    got = both(acts, acts)
    held = back(where, (0,), (acts,), w, None, ring)
    for k in (1, 2, 3):
        now = got
        if k < 3:
            got = both(*now)
        else:
            got = both(now[0][:half], now[1][half:])
        held = back(where, (-k, k,), now, w, held, ring)
    early = lax.ppermute(held[1], "core", swap)
    keep, send, acts = back(where, (4,), got, w, held, ring, halves=True)
    late = lax.ppermute(send, "core", swap)
    sums = join(where, held[0], early, keep, late)
    sums = lax.all_to_all(sums, ("x", "ylo"), 0, 0, tiled=True)
    lanes = 128
    own = call(
        split_kernel,
        grid=(depth // lanes,),
        in_specs=[pl.BlockSpec((n_chips, height, lanes), lambda i: (0, 0, i))],
        out_specs=pl.BlockSpec((2 * experts, slots, lanes), lambda i: (0, 0, i)),
        out_shape=jax.ShapeDtypeStruct((2 * experts, slots, depth), BF16),
    )(sums)
    returned = lax.all_to_all(own, ("core", "expert"), 0, 0, tiled=True)
    out, d_tokens = call(
        finish_kernel,
        out_shape=[jax.ShapeDtypeStruct(tokens.shape, BF16)] * 2,
    )(ids_row, gates_row, returned)

    acts = acts.reshape(ring * height, 3 * width)
    x = jnp.where(core == 0, mine, other).reshape(n_chips * height, depth)
    dy = jnp.where(core == 0, other, mine).reshape(n_chips * height, depth)
    grads = [
        contract_rows(x if a < 2 else dy, acts[:, a * width : (a + 1) * width]).astype(BF16)[None]
        for a in range(3)
    ]
    return (out, d_tokens, *grads)


def solution(mesh):
    fine = Mesh(
        mesh.devices.reshape(2, 4, 2, 4, 8), ("ylo", "x", "core", "expert", "tensor")
    )
    dp = ("ylo", "x", "core")
    tok = P((*dp, "expert"), "tensor")
    route = P((*dp, "expert"), None)
    saved = P(None, "tensor", (*dp, "expert"))
    grad = P("expert", "tensor", dp)
    return jax.shard_map(
        step,
        mesh=fine,
        in_specs=(tok, route, route, tok, saved, saved, saved),
        out_specs=(tok, tok, grad, grad, grad),
        check_vma=False,
    )
```
